128 devices in a mesh: front: 16 (over y, x_lo, core), blk: 8 (over x_hi, z).
Axes of the slice: x: 4 (x_hi: 2, x_lo: 2; x = x_hi * 2 + x_lo), y: 4, z: 4, core: 2. Of those that a mesh axis runs over, the one named last changes fastest.
Arguments:
- factor_rows: float32 [16, 4096, 1024], P('front', 'blk'), may hold values from -0.375 to 0.375
- front_sizes: int32 [16], P('front'), may hold values from 4 to 8
- tile_counts: int32 [16], replicated, may hold values from 29 to 32
- parent_tiles: int32 [16, 32, 32], replicated, may hold values from 0 to 1023, as said below
- parent_entries: float32 [1024, 128, 128], P(('front', 'blk')), may hold values from -6 to 6
Outputs:
- parent_update: float32 [1024, 128, 128], P(('front', 'blk'))
The draws below stay inside these ranges and needn't reach their ends.
Inputs may be any that keep to these rules, and one draw needn't show every extreme that they name: `parent_tiles`: parent tile p is owned by the device of linear index p // 8 over front and blk (front slowest). Among the tiles of the rows of one device (its 4 index blocks of rows, all 32 columns), no owner is named more than 2 times; one owner is named exactly 2 times by every device, by tiles of the device's first row block in columns below 2.
All inputs are finite; a program needn't handle non-finite values.
Results may differ from the reference program's by a relative error of at most 0.0003.
Values sent between devices are 32-bit elements; how exact they have to be, the bound alone decides.
A program may use at most 128 MiB of HBM per device.

```python
import jax
import jax.numpy as jnp
from jax import lax

K = 1024
TR = 128
RB = 4
PT_DEV = 8
KT = 8
EB = 32
EROWS = 4096
CAP = 2
PTILES = 1024
N_FRONT = 16
N_BLK = 8


def draw_parent_tiles(key, part):
    devices = N_FRONT * N_BLK
    tile_total = RB * EB
    key_hot, key_shuffle, key_local = jax.random.split(key, 3)
    hot_owner = jax.random.randint(key_hot, (), 0, devices, dtype=jnp.int32)
    slot_pool = jnp.arange((devices - 1) * CAP, dtype=jnp.int32) // CAP
    slot_pool = slot_pool + (slot_pool >= hot_owner).astype(jnp.int32)
    device_keys = jax.random.split(key_shuffle, devices)

    def draw_device(dev_key):
        shuffle = jax.random.permutation(dev_key, (devices - 1) * CAP)
        return slot_pool[shuffle[:tile_total - CAP]]
    others = jax.vmap(draw_device)(device_keys)
    owners = jnp.concatenate([jnp.full((devices, CAP), hot_owner, jnp.int32), others], axis=1)
    local_slot = jax.random.randint(key_local, (devices, tile_total), 0, PT_DEV, dtype=jnp.int32)
    tile_ids = owners * PT_DEV + local_slot
    return tile_ids.reshape(N_FRONT, EB, EB)


def place_ends(drawn, rng, low, largest):
    dims = drawn.shape
    spot = [jax.random.randint(jax.random.fold_in(rng, axis), (), 0, dims[axis]) for axis in range(len(dims))]
    drawn = drawn.at[tuple(spot)].set(low)
    longest = dims.index(max(dims))
    spot[longest] = (spot[longest] + 1) % dims[longest]
    return drawn.at[tuple(spot)].set(largest)


def levels(key, extent, shards, least, high):
    factor_of = 1.0
    for dim, shards_of in shards:
        heights = jax.random.uniform(jax.random.fold_in(jax.random.fold_in(key, 6), dim), (shards_of,), jnp.float32, least / len(shards), high / len(shards))
        factor_of = factor_of * jnp.repeat(jnp.exp(heights), extent[dim] // shards_of).reshape((-1,) + (1,) * (len(extent) - 1 - dim))
    return factor_of


def centred(stream_key, extent, deviation, limit, cuts=(), kind=jnp.bfloat16):
    drawn = deviation * jax.random.normal(stream_key, extent, jnp.float32)
    if cuts:
        drawn = drawn * levels(stream_key, extent, cuts, -0.22, 0.18)
    return jnp.clip(drawn, -limit, limit).astype(kind)


def setup_inputs(seed: int = 0) -> dict:
    seeds = jax.random.split(jax.random.key(seed), 6)
    return {
        "factor_rows": centred(seeds[0], (N_FRONT, EROWS, K), (K // 4) ** -0.5, 0.375, ((0, 16), (1, 8)), jnp.float32),
        "front_sizes": place_ends(jax.random.randint(seeds[1], (N_FRONT,), KT // 2, KT + 1), jax.random.fold_in(seeds[1], 1), KT // 2, KT).astype(jnp.int32),
        "tile_counts": place_ends(jax.random.randint(seeds[2], (N_FRONT,), EB - max(RB, 2) + 1, EB + 1), jax.random.fold_in(seeds[2], 1), EB - max(RB, 2) + 1, EB).astype(jnp.int32),
        "parent_tiles": draw_parent_tiles(jax.random.fold_in(seeds[5], 71), 0),
        "parent_entries": centred(seeds[4], (PTILES, TR, TR), 0.5, 6.0, ((0, 128),), jnp.float32),
    }


def reference(factor_rows, front_sizes, tile_counts, parent_tiles, parent_entries):
    column_ids = jnp.arange(K, dtype=jnp.int32)
    block_ids = jnp.arange(EB, dtype=jnp.int32)

    def add_group(running, inputs):
        group_rows, pivots, live_count, targets = inputs
        masked = jnp.where((column_ids < pivots * TR)[None, :], group_rows, 0.0)
        schur_full = jnp.dot(masked, masked.T, precision=lax.Precision.HIGHEST, preferred_element_type=jnp.float32)
        tile_stack = schur_full.reshape(EB, TR, EB, TR).transpose(0, 2, 1, 3).reshape(EB * EB, TR, TR)
        live_mask = (block_ids[:, None] < live_count) & (block_ids[None, :] < live_count)
        tile_stack = jnp.where(live_mask.reshape(-1)[:, None, None], tile_stack, 0.0)
        added = jax.ops.segment_sum(tile_stack, targets.reshape(-1).astype(jnp.int32), num_segments=PTILES)
        return running + added, None

    start = jnp.zeros((PTILES, TR, TR), jnp.float32)
    running, _ = lax.scan(add_group, start, (factor_rows, front_sizes, tile_counts, parent_tiles))
    return parent_entries - running
```

```python
import functools

import jax
import jax.numpy as jnp
from jax import lax
from jax.experimental import pallas as pl
from jax.experimental.pallas import tpu as pltpu
from jax.sharding import PartitionSpec as P

TR = 128
KH = 512
CB = 4
EB = 32
UNROLL = 4

MESH = pl.DeviceIdType.MESH
F32 = jnp.float32
BF16 = jnp.bfloat16


def position():
    front, blk = lax.axis_index("front"), lax.axis_index("blk")
    return dict(
        front=front,
        blk=blk,
        y=front // 4,
        xl=(front // 2) % 2,
        core=front % 2,
        xh=blk // 4,
        z=blk % 4,
    )


def device(p, **moves):
    q = {**p, **moves}
    return {"front": q["y"] * 4 + q["xl"] * 2 + q["core"], "blk": q["xh"] * 4 + q["z"]}


def slot(xs, dz, c):
    return (xs * 4 + dz) * CB + c


def gather_kernel(
    x, parents, fs, counts, hl, lists, tile_counts,
    mine, other, split, fs_other,
    x_send, z_send, recv, core_send, core_recv, local, out_sem, fs_sem,
):
    p = position()
    z, xh = p["z"], p["xh"]
    up, down = device(p, z=(z + 1) % 4), device(p, z=(z + 3) % 4)
    across = device(p, xh=1 - xh)
    twin = device(p, core=1 - p["core"])

    barrier = pltpu.get_barrier_semaphore()
    for other_dev in (up, down, across, twin):
        pl.semaphore_signal(barrier, inc=1, device_id=other_dev, device_id_type=MESH)
    pl.semaphore_wait(barrier, 4)

    sent = []
    ready = []

    def send(src, dst, ssem, rsem, to):
        copy = pltpu.make_async_remote_copy(
            src_ref=src, dst_ref=dst, send_sem=ssem, recv_sem=rsem, device_id=to, device_id_type=MESH
        )
        copy.start()
        sent.append(copy)

    n_z = [0]

    def send_z(src, xs, dz, c, to):
        s = slot(xs, dz, c)
        send(src, mine.at[s], z_send.at[n_z[0]], recv.at[s], to)
        n_z[0] += 1

    def arrived(s):
        pltpu.make_async_remote_copy(
            src_ref=mine.at[s], dst_ref=mine.at[s], send_sem=z_send.at[0], recv_sem=recv.at[s],
            device_id=up, device_id_type=MESH,
        ).wait_recv()

    def to_twin(s):
        send(mine.at[s], other.at[s], core_send.at[s], core_recv.at[s], twin)

    def from_twin(s):
        pltpu.make_async_remote_copy(
            src_ref=mine.at[s], dst_ref=other.at[s], send_sem=core_send.at[s], recv_sem=core_recv.at[s],
            device_id=twin, device_id_type=MESH,
        ).wait_recv()

    own_cols = pl.ds(pl.multiple_of(xh * KH, KH), KH)
    across_cols = pl.ds(pl.multiple_of((1 - xh) * KH, KH), KH)

    def rows(c):
        return pl.ds(c * TR, TR)

    send(fs, fs_other, fs_sem.at[0], fs_sem.at[1], twin)
    fs_copy = sent[-1]
    loads = []
    for c in (0, 2, 1, 3):
        s = slot(1, 0, c)
        send(x.at[rows(c), across_cols], mine.at[s], x_send.at[c], recv.at[s], across)
    for c, d in ((0, 2), (1, 3), (2, 0), (3, 1)):
        send_z(x.at[rows(c), own_cols], 0, 3, c, up)
        send_z(x.at[rows(d), own_cols], 0, 1, d, down)
        load = pltpu.make_async_copy(x.at[rows(c), own_cols], mine.at[slot(0, 0, c)], local.at[c])
        load.start()
        loads.append(load)

    col = lax.broadcasted_iota(jnp.int32, (EB, EB), 1)
    row = lax.broadcasted_iota(jnp.int32, (EB, EB), 0)
    lower = (row >= col).astype(F32)
    for g in range(2):
        f = (p["front"] // 2) * 2 + (p["core"] if g == 0 else 1 - p["core"])
        target = parents[f]
        live = counts[f][0:1, 0:EB]
        dest = target >> 3
        dest_front, dest_blk = dest >> 3, dest & 7
        hit = ((dest_blk & 3) == z) & ((dest_front & 1) == p["core"])
        hit = hit & (row < live) & (col < live)
        rx = ((dest_blk >> 2) * 2 + ((dest_front >> 1) & 1) - (p["xh"] * 2 + p["xl"])) & 3
        ry = ((dest_front >> 2) - p["y"]) & 3
        place = target & 7
        first = place < 4
        at = jnp.where(first, ry * 4 + rx, 16 + rx * 4 + ry) * 4 + (place & 3)
        code = (col << 13) + (row << 8) + at
        rank = jnp.dot(lower, hit.astype(F32), preferred_element_type=F32).astype(jnp.int32)
        tile_counts[g : g + 1, 0:EB] = rank[EB - 1 : EB, :]
        rank = jnp.where(hit, rank, 0)
        for k in range(EB):
            lists[g, k : k + 1, 0:EB] = jnp.sum(jnp.where(rank == k + 1, code, 0), axis=0, keepdims=True)

    def convert(g, s):
        src = mine if g == 0 else other
        size = (fs if g == 0 else fs_other)[0:1, :]
        block = lax.broadcasted_iota(jnp.int32, (1, KH), 1) // TR + xh * (KH // TR)
        keep = block < size

        def step(i, _):
            at = pl.multiple_of(i * 16, 16)
            v = jnp.where(keep, src[s, pl.ds(at, 16), :], 0.0)
            hi = v.astype(BF16)
            split[g, s, pl.ds(at, 16), :] = hi
            split[g, s, pl.ds(TR + at, 16), :] = (v - hi.astype(F32)).astype(BF16)
            return 0

        lax.fori_loop(0, TR // 16, step, 0)
        ready.append((g, s))

    outs = []

    def put():
        g, s = ready.pop(0)
        xs, dz, c = s // 16, (s // 4) % 4, s % 4
        blk = (xh if xs == 0 else 1 - xh) * 4 + (z + dz) % 4
        copy = pltpu.make_async_copy(split.at[g, s], hl.at[g, blk * CB + c], out_sem.at[g * 32 + s])
        copy.start()
        outs.append(copy)

    twin_queue = []

    def take(s):
        to_twin(s)
        convert(0, s)
        twin_queue.append(s)
        if len(ready) > 1:
            put()
        if len(twin_queue) > 4:
            drain()

    def drain():
        t = twin_queue.pop(0)
        from_twin(t)
        convert(1, t)
        if len(ready) > 1:
            put()

    fs_copy.wait_recv()
    for c, load in zip((0, 1, 2, 3), loads):
        load.wait()
        take(slot(0, 0, c))
    for i in range(4):
        c, d = (0, 1, 2, 3)[i], (2, 3, 0, 1)[i]
        arrived(slot(0, 3, c))
        if c < 2:
            send_z(mine.at[slot(0, 3, c)], 0, 2, c, up)
        take(slot(0, 3, c))
        arrived(slot(0, 1, d))
        if d >= 2:
            send_z(mine.at[slot(0, 1, d)], 0, 2, d, down)
        take(slot(0, 1, d))
        e = (0, 2, 1, 3)[i]
        s = slot(1, 0, e)
        arrived(s)
        send_z(mine.at[s], 1, 3, e, up)
        send_z(mine.at[s], 1, 1, e, down)
        take(s)
    for e in (0, 2, 1, 3):
        arrived(slot(0, 2, e))
        take(slot(0, 2, e))
    for e in (0, 2, 1, 3):
        s = slot(1, 3, e)
        arrived(s)
        if e < 2:
            send_z(mine.at[s], 1, 2, e, up)
        take(s)
        s = slot(1, 1, e)
        arrived(s)
        if e >= 2:
            send_z(mine.at[s], 1, 2, e, down)
        take(s)
    for e in (0, 2, 1, 3):
        arrived(slot(1, 2, e))
        take(slot(1, 2, e))
    while twin_queue:
        drain()
    while ready:
        put()
    for copy in sent:
        copy.wait_send()
    for copy in outs:
        copy.wait()


def tiles_kernel(lists, counts, hl, out, held, acc, flat, load_sem, out_sem):
    loads = []
    for g in range(2):
        for q in range(4):
            part = pl.ds(q * 8, 8)
            load = pltpu.make_async_copy(hl.at[g, part], held.at[g, part], load_sem.at[g * 4 + q])
            load.start()
            loads.append(load)

    def clear(i, _):
        acc[i] = jnp.zeros((TR, TR), F32)
        return 0

    lax.fori_loop(0, 129, clear, 0)

    totals = []
    for g in range(2):
        def column(b, n):
            def entry(k, n):
                flat[g, n] = lists[g, k, b]
                return n + 1

            return lax.fori_loop(0, counts[g, b], entry, n)

        n = lax.fori_loop(0, EB, column, 0)
        for u in range(UNROLL - 1):
            flat[g, n + u] = 128
        totals.append(n)

    for g in range(2):
        for q in range(4):
            loads[g * 4 + q].wait()

        def several(i, _):
            for u in range(UNROLL):
                code = flat[g, i * UNROLL + u]
                b, a, at = code >> 13, (code >> 8) & 31, code & 255
                d = lax.dot_general(
                    held[g, a], held[g, b], (((1,), (1,)), ((), ())), preferred_element_type=F32
                )
                acc[at] += d[:TR, :TR] + (d[:TR, TR:] + d[TR:, :TR])
            return 0

        lax.fori_loop(0, (totals[g] + UNROLL - 1) // UNROLL, several, 0)

    copy = pltpu.make_async_copy(acc.at[pl.ds(0, 128)], out, out_sem)
    copy.start()
    copy.wait()


def scatter_kernel(
    part, out, data, opp, near, fwd, mid, mid_opp, mid_near, mid_fwd, res,
    send_sem, recv_sem, load_sem,
):
    p = position()
    x = p["xh"] * 2 + p["xl"]

    def along_x(d):
        n = (x + d) % 4
        return device(p, xh=n // 2, xl=n % 2)

    def along_y(d):
        return device(p, y=(p["y"] + d) % 4)

    barrier = pltpu.get_barrier_semaphore()
    for to in (along_x(1), along_x(3), along_y(1), along_y(3)):
        pl.semaphore_signal(barrier, inc=1, device_id=to, device_id_type=MESH)
    pl.semaphore_wait(barrier, 4)

    sent = []
    count = [0]

    def send(src, dst, to):
        k = count[0]
        count[0] += 1
        copy = pltpu.make_async_remote_copy(
            src_ref=src, dst_ref=dst, send_sem=send_sem.at[k], recv_sem=recv_sem.at[k],
            device_id=to, device_id_type=MESH,
        )
        copy.start()
        sent.append(copy)
        return copy

    def begin(src, n, h, to, opp, near):
        half = n // 2
        o_up = send(src(2, 0, half), opp.at[h, 0], to(1))
        o_down = send(src(2, half, half), opp.at[h, 1], to(3))
        n_up = send(src(1, half, half), near.at[h, 0, pl.ds(half, half)], to(1))
        n_down = send(src(3, 0, half), near.at[h, 1, pl.ds(0, half)], to(3))
        return o_up, o_down, n_up, n_down

    def relay(copies, val, n, h, to, opp, near, fwd):
        half = n // 2
        copies[0].wait_recv()
        fwd[h, 0] = val(1, 0, half) + opp[h, 0]
        f_up = send(fwd.at[h, 0], near.at[h, 0, pl.ds(0, half)], to(1))
        copies[1].wait_recv()
        fwd[h, 1] = val(3, half, half) + opp[h, 1]
        f_down = send(fwd.at[h, 1], near.at[h, 1, pl.ds(half, half)], to(3))
        return copies[2], copies[3], f_up, f_down

    ways = ((along_y, along_x), (along_x, along_y))
    firsts = []
    for h in range(2):
        firsts.append(
            begin(lambda r, lo, size: part.at[pl.ds(h * 64 + r * 16 + lo, size)], 16, h, ways[h][0], opp, near)
        )
    loads = []
    for h in range(2):
        for r in (1, 3, 0):
            sl = pl.ds(h * 64 + r * 16, 16)
            load = pltpu.make_async_copy(part.at[sl], data.at[sl], load_sem.at[h * 4 + r])
            load.start()
            loads.append(load)
    for load in loads:
        load.wait()

    seconds = []
    for h in range(2):
        firsts[h] = relay(
            firsts[h], lambda r, lo, size: data[pl.ds(h * 64 + r * 16 + lo, size)], 16, h, ways[h][0], opp, near, fwd
        )
    for h in range(2):
        for copy in firsts[h]:
            copy.wait_recv()
        mid[h] = data[pl.ds(h * 64, 16)] + (near[h, 0] + near[h, 1])
        seconds.append(
            begin(lambda r, lo, size: mid.at[h, pl.ds(r * 4 + lo, size)], 4, h, ways[h][1], mid_opp, mid_near)
        )
    for h in range(2):
        seconds[h] = relay(
            seconds[h], lambda r, lo, size: mid[h, pl.ds(r * 4 + lo, size)], 4, h, ways[h][1], mid_opp, mid_near, mid_fwd
        )
    for h in range(2):
        for copy in seconds[h]:
            copy.wait_recv()
        out[pl.ds(h * 4, 4)] = mid[h, pl.ds(0, 4)] + (mid_near[h, 0] + mid_near[h, 1])
    for copy in sent:
        copy.wait_send()


def per_device(factor_rows, front_sizes, tile_counts, parent_tiles, parent_entries):
    any_space = pl.BlockSpec(memory_space=pl.ANY)
    vmem = pl.BlockSpec(memory_space=pltpu.VMEM)
    limit = 60 * 2**20
    fs = jnp.broadcast_to(front_sizes.reshape(1, 1), (8, KH))
    live = jnp.broadcast_to(tile_counts[:, None, None], (16, 8, 128))
    dma = pltpu.SemaphoreType.DMA
    hl, lists, counts = pl.pallas_call(
        gather_kernel,
        out_shape=(
            jax.ShapeDtypeStruct((2, EB, 2 * TR, KH), BF16),
            jax.ShapeDtypeStruct((2, EB, 128), jnp.int32),
            jax.ShapeDtypeStruct((8, 128), jnp.int32),
        ),
        in_specs=[any_space, vmem, vmem, vmem],
        out_specs=(any_space, vmem, vmem),
        scratch_shapes=[
            pltpu.VMEM((EB, TR, KH), F32),
            pltpu.VMEM((EB, TR, KH), F32),
            pltpu.VMEM((2, EB, 2 * TR, KH), BF16),
            pltpu.VMEM((8, KH), jnp.int32),
            dma((4,)),
            dma((24,)),
            dma((32,)),
            dma((32,)),
            dma((32,)),
            dma((4,)),
            dma((64,)),
            dma((2,)),
        ],
        compiler_params=pltpu.CompilerParams(collective_id=0, has_side_effects=True, vmem_limit_bytes=limit),
        name="gather",
    )(factor_rows[0], parent_tiles, fs, live)
    part = pl.pallas_call(
        tiles_kernel,
        out_shape=jax.ShapeDtypeStruct((128, TR, TR), F32),
        grid_spec=pltpu.PrefetchScalarGridSpec(
            num_scalar_prefetch=2,
            grid=(1,),
            in_specs=[any_space],
            out_specs=any_space,
            scratch_shapes=[
                pltpu.VMEM((2, EB, 2 * TR, KH), BF16),
                pltpu.VMEM((129, TR, TR), F32),
                pltpu.SMEM((2, 1024 + 128), jnp.int32),
                dma((8,)),
                dma,
            ],
        ),
        compiler_params=pltpu.CompilerParams(vmem_limit_bytes=limit),
        name="tiles",
    )(lists[:, :, :EB], counts[:2, :EB], hl)
    summed = pl.pallas_call(
        scatter_kernel,
        out_shape=jax.ShapeDtypeStruct((8, TR, TR), F32),
        in_specs=[any_space],
        out_specs=vmem,
        scratch_shapes=[
            pltpu.VMEM((128, TR, TR), F32),
            pltpu.VMEM((2, 2, 8, TR, TR), F32),
            pltpu.VMEM((2, 2, 16, TR, TR), F32),
            pltpu.VMEM((2, 2, 8, TR, TR), F32),
            pltpu.VMEM((2, 16, TR, TR), F32),
            pltpu.VMEM((2, 2, 2, TR, TR), F32),
            pltpu.VMEM((2, 2, 4, TR, TR), F32),
            pltpu.VMEM((2, 2, 2, TR, TR), F32),
            pltpu.VMEM((8, TR, TR), F32),
            dma((24,)),
            dma((24,)),
            dma((8,)),
        ],
        compiler_params=pltpu.CompilerParams(collective_id=1, has_side_effects=True, vmem_limit_bytes=limit),
        name="scatter",
    )(part)
    return parent_entries - summed


def solution(mesh):
    in_specs = (P("front", "blk", None), P("front"), P(), P(), P(("front", "blk"), None, None))
    out_specs = P(("front", "blk"), None, None)
    return jax.shard_map(
        per_device, mesh=mesh, in_specs=in_specs, out_specs=out_specs, check_vma=False
    )
```

```python
import functools

import jax
import jax.numpy as jnp
from jax import lax
from jax.experimental import pallas as pl
from jax.experimental.pallas import tpu as pltpu
from jax.sharding import PartitionSpec as P

TR = 128
KH = 512
CB = 4
EB = 32
UNROLL = 16

MESH = pl.DeviceIdType.MESH
F32 = jnp.float32
BF16 = jnp.bfloat16


def position():
    front, blk = lax.axis_index("front"), lax.axis_index("blk")
    return dict(
        front=front,
        blk=blk,
        y=front // 4,
        xl=(front // 2) % 2,
        core=front % 2,
        xh=blk // 4,
        z=blk % 4,
    )


def device(p, **moves):
    q = {**p, **moves}
    return {"front": q["y"] * 4 + q["xl"] * 2 + q["core"], "blk": q["xh"] * 4 + q["z"]}


def slot(xs, dz, c):
    return (xs * 4 + dz) * CB + c


def gather_kernel(
    x, parents, sizes, counts, split, lists, tile_counts,
    mine, other, fs, fs_other,
    x_send, z_send, recv, core_send, core_recv, local, fs_sem,
):
    p = position()
    z, xh = p["z"], p["xh"]
    up, down = device(p, z=(z + 1) % 4), device(p, z=(z + 3) % 4)
    across = device(p, xh=1 - xh)
    twin = device(p, core=1 - p["core"])

    fs[...] = jnp.full((8, KH), sizes[0], jnp.int32)
    barrier = pltpu.get_barrier_semaphore()
    for other_dev in (up, down, across, twin):
        pl.semaphore_signal(barrier, inc=1, device_id=other_dev, device_id_type=MESH)
    pl.semaphore_wait(barrier, 4)

    sent = []

    def send(src, dst, ssem, rsem, to):
        copy = pltpu.make_async_remote_copy(
            src_ref=src, dst_ref=dst, send_sem=ssem, recv_sem=rsem, device_id=to, device_id_type=MESH
        )
        copy.start()
        sent.append(copy)

    n_z = [0]

    def send_z(src, xs, dz, c, to):
        s = slot(xs, dz, c)
        send(src, mine.at[s], z_send.at[n_z[0]], recv.at[s], to)
        n_z[0] += 1

    def arrived(s):
        pltpu.make_async_remote_copy(
            src_ref=mine.at[s], dst_ref=mine.at[s], send_sem=z_send.at[0], recv_sem=recv.at[s],
            device_id=up, device_id_type=MESH,
        ).wait_recv()

    def to_twin(s):
        send(mine.at[s], other.at[s], core_send.at[s], core_recv.at[s], twin)

    def from_twin(s):
        pltpu.make_async_remote_copy(
            src_ref=mine.at[s], dst_ref=other.at[s], send_sem=core_send.at[s], recv_sem=core_recv.at[s],
            device_id=twin, device_id_type=MESH,
        ).wait_recv()

    own_cols = pl.ds(pl.multiple_of(xh * KH, KH), KH)
    across_cols = pl.ds(pl.multiple_of((1 - xh) * KH, KH), KH)

    def rows(c):
        return pl.ds(c * TR, TR)

    send(fs, fs_other, fs_sem.at[0], fs_sem.at[1], twin)
    fs_copy = sent[-1]
    loads = []
    for c in (0, 2, 1, 3):
        s = slot(1, 0, c)
        send(x.at[rows(c), across_cols], mine.at[s], x_send.at[c], recv.at[s], across)
    for c, d in ((0, 2), (1, 3), (2, 0), (3, 1)):
        send_z(x.at[rows(c), own_cols], 0, 3, c, up)
        send_z(x.at[rows(d), own_cols], 0, 1, d, down)
        load = pltpu.make_async_copy(x.at[rows(c), own_cols], mine.at[slot(0, 0, c)], local.at[c])
        load.start()
        loads.append(load)

    col = lax.broadcasted_iota(jnp.int32, (EB, EB), 1)
    row = lax.broadcasted_iota(jnp.int32, (EB, EB), 0)
    lower = (row >= col).astype(F32)

    def place_of(block):
        return ((((block >> 4) ^ xh) << 4) + ((((block >> 2) - z) & 3) << 2)) + (block & 3)

    for g in range(2):
        f = (p["front"] // 2) * 2 + (p["core"] if g == 0 else 1 - p["core"])
        target = parents[f]
        live = counts[f]
        dest = target >> 3
        dest_front, dest_blk = dest >> 3, dest & 7
        hit = ((dest_blk & 3) == z) & ((dest_front & 1) == p["core"])
        hit = hit & (row < live) & (col < live)
        rx = ((dest_blk >> 2) * 2 + ((dest_front >> 1) & 1) - (p["xh"] * 2 + p["xl"])) & 3
        ry = ((dest_front >> 2) - p["y"]) & 3
        place = target & 7
        first = place < 4
        at = jnp.where(first, ry * 4 + rx, 16 + rx * 4 + ry) * 4 + (place & 3)
        code = (place_of(col) << 13) + (place_of(row) << 8) + at
        rank = jnp.dot(lower, hit.astype(F32), preferred_element_type=F32).astype(jnp.int32)
        tile_counts[g : g + 1, 0:EB] = rank[EB - 1 : EB, :]
        rank = jnp.where(hit, rank, 0)
        for k in range(EB):
            lists[g, k : k + 1, 0:EB] = jnp.sum(jnp.where(rank == k + 1, code, 0), axis=0, keepdims=True)

    def convert(g, s):
        src = mine if g == 0 else other
        size = (fs if g == 0 else fs_other)[0:1, :]
        block = lax.broadcasted_iota(jnp.int32, (1, KH), 1) // TR + xh * (KH // TR)
        keep = block < size

        def step(i, _):
            at = pl.multiple_of(i * 16, 16)
            v = jnp.where(keep, src[s, pl.ds(at, 16), :], 0.0)
            hi = v.astype(BF16)
            split[g, s, pl.ds(at, 16), :] = hi
            split[g, s, pl.ds(TR + at, 16), :] = (v - hi.astype(F32)).astype(BF16)
            return 0

        lax.fori_loop(0, TR // 16, step, 0)

    twin_queue = []

    def take(s):
        to_twin(s)
        convert(0, s)
        twin_queue.append(s)
        if len(twin_queue) > 4:
            drain()

    def drain():
        t = twin_queue.pop(0)
        from_twin(t)
        convert(1, t)

    fs_copy.wait_recv()
    for c, load in zip((0, 1, 2, 3), loads):
        load.wait()
        take(slot(0, 0, c))
    for i in range(4):
        c, d = (0, 1, 2, 3)[i], (2, 3, 0, 1)[i]
        arrived(slot(0, 3, c))
        if c < 2:
            send_z(mine.at[slot(0, 3, c)], 0, 2, c, up)
        take(slot(0, 3, c))
        arrived(slot(0, 1, d))
        if d >= 2:
            send_z(mine.at[slot(0, 1, d)], 0, 2, d, down)
        take(slot(0, 1, d))
        e = (0, 2, 1, 3)[i]
        s = slot(1, 0, e)
        arrived(s)
        send_z(mine.at[s], 1, 3, e, up)
        send_z(mine.at[s], 1, 1, e, down)
        take(s)
    for e in (0, 2, 1, 3):
        arrived(slot(0, 2, e))
        take(slot(0, 2, e))
    for e in (0, 2, 1, 3):
        s = slot(1, 3, e)
        arrived(s)
        if e < 2:
            send_z(mine.at[s], 1, 2, e, up)
        take(s)
        s = slot(1, 1, e)
        arrived(s)
        if e >= 2:
            send_z(mine.at[s], 1, 2, e, down)
        take(s)
    for e in (0, 2, 1, 3):
        arrived(slot(1, 2, e))
        take(slot(1, 2, e))
    while twin_queue:
        drain()
    for copy in sent:
        copy.wait_send()


def tiles_kernel(lists, counts, held, acc, flat):
    def clear(i, _):
        acc[i] = jnp.zeros((TR, TR), F32)
        return 0

    lax.fori_loop(0, 129, clear, 0)

    totals = []
    for g in range(2):
        def column(b, n):
            def entry(k, n):
                flat[g, n] = lists[g, k, b]
                return n + 1

            return lax.fori_loop(0, counts[g, b], entry, n)

        n = lax.fori_loop(0, EB, column, 0)
        for u in range(UNROLL - 1):
            flat[g, n + u] = 128
        totals.append(n)

    for g in range(2):
        def several(i, _):
            for u in range(UNROLL):
                code = flat[g, i * UNROLL + u]
                b, a, at = code >> 13, (code >> 8) & 31, code & 255
                d = lax.dot_general(
                    held[g, a], held[g, b], (((1,), (1,)), ((), ())), preferred_element_type=F32
                )
                acc[at] += d[:TR, :TR] + (d[:TR, TR:] + d[TR:, :TR])
            return 0

        lax.fori_loop(0, (totals[g] + UNROLL - 1) // UNROLL, several, 0)


def scatter_kernel(
    part, out, opp, near, fwd, mid, mid_opp, mid_near, mid_fwd,
    send_sem, recv_sem,
):
    p = position()
    x = p["xh"] * 2 + p["xl"]

    def along_x(d):
        n = (x + d) % 4
        return device(p, xh=n // 2, xl=n % 2)

    def along_y(d):
        return device(p, y=(p["y"] + d) % 4)

    barrier = pltpu.get_barrier_semaphore()
    for to in (along_x(1), along_x(3), along_y(1), along_y(3)):
        pl.semaphore_signal(barrier, inc=1, device_id=to, device_id_type=MESH)
    pl.semaphore_wait(barrier, 4)

    sent = []
    count = [0]

    def send(src, dst, to):
        k = count[0]
        count[0] += 1
        copy = pltpu.make_async_remote_copy(
            src_ref=src, dst_ref=dst, send_sem=send_sem.at[k], recv_sem=recv_sem.at[k],
            device_id=to, device_id_type=MESH,
        )
        copy.start()
        sent.append(copy)
        return copy

    def begin(src, n, h, to, opp, near):
        half = n // 2
        o_up = send(src(2, 0, half), opp.at[h, 0], to(1))
        o_down = send(src(2, half, half), opp.at[h, 1], to(3))
        n_up = send(src(1, half, half), near.at[h, 0, pl.ds(half, half)], to(1))
        n_down = send(src(3, 0, half), near.at[h, 1, pl.ds(0, half)], to(3))
        return o_up, o_down, n_up, n_down

    def relay(copies, val, n, h, to, opp, near, fwd):
        half = n // 2
        copies[0].wait_recv()
        fwd[h, 0] = val(1, 0, half) + opp[h, 0]
        f_up = send(fwd.at[h, 0], near.at[h, 0, pl.ds(0, half)], to(1))
        copies[1].wait_recv()
        fwd[h, 1] = val(3, half, half) + opp[h, 1]
        f_down = send(fwd.at[h, 1], near.at[h, 1, pl.ds(half, half)], to(3))
        return copies[2], copies[3], f_up, f_down

    ways = ((along_y, along_x), (along_x, along_y))
    firsts = []
    for h in range(2):
        firsts.append(
            begin(lambda r, lo, size: part.at[pl.ds(h * 64 + r * 16 + lo, size)], 16, h, ways[h][0], opp, near)
        )
    seconds = []
    for h in range(2):
        firsts[h] = relay(
            firsts[h], lambda r, lo, size: part[pl.ds(h * 64 + r * 16 + lo, size)], 16, h, ways[h][0], opp, near, fwd
        )
    for h in range(2):
        for copy in firsts[h]:
            copy.wait_recv()
        mid[h] = part[pl.ds(h * 64, 16)] + (near[h, 0] + near[h, 1])
        seconds.append(
            begin(lambda r, lo, size: mid.at[h, pl.ds(r * 4 + lo, size)], 4, h, ways[h][1], mid_opp, mid_near)
        )
    for h in range(2):
        seconds[h] = relay(
            seconds[h], lambda r, lo, size: mid[h, pl.ds(r * 4 + lo, size)], 4, h, ways[h][1], mid_opp, mid_near, mid_fwd
        )
    for h in range(2):
        for copy in seconds[h]:
            copy.wait_recv()
        out[pl.ds(h * 4, 4)] = mid[h, pl.ds(0, 4)] + (mid_near[h, 0] + mid_near[h, 1])
    for copy in sent:
        copy.wait_send()


def per_device(factor_rows, front_sizes, tile_counts, parent_tiles, parent_entries):
    any_space = pl.BlockSpec(memory_space=pl.ANY)
    vmem = pl.BlockSpec(memory_space=pltpu.VMEM)
    smem = pl.BlockSpec(memory_space=pltpu.SMEM)
    dma = pltpu.SemaphoreType.DMA
    split, lists, counts = pl.pallas_call(
        gather_kernel,
        out_shape=(
            jax.ShapeDtypeStruct((2, EB, 2 * TR, KH), BF16),
            jax.ShapeDtypeStruct((2, EB, 128), jnp.int32),
            jax.ShapeDtypeStruct((8, 128), jnp.int32),
        ),
        in_specs=[any_space, vmem, smem, smem],
        out_specs=(vmem, vmem, vmem),
        scratch_shapes=[
            pltpu.VMEM((EB, TR, KH), F32),
            pltpu.VMEM((EB, TR, KH), F32),
            pltpu.VMEM((8, KH), jnp.int32),
            pltpu.VMEM((8, KH), jnp.int32),
            dma((4,)),
            dma((24,)),
            dma((32,)),
            dma((32,)),
            dma((32,)),
            dma((4,)),
            dma((2,)),
        ],
        compiler_params=pltpu.CompilerParams(collective_id=0, has_side_effects=True, vmem_limit_bytes=20 * 2**20),
        name="gather",
    )(factor_rows[0], parent_tiles, front_sizes, tile_counts)
    part = pl.pallas_call(
        tiles_kernel,
        out_shape=jax.ShapeDtypeStruct((129, TR, TR), F32),
        in_specs=[smem, smem, vmem],
        out_specs=vmem,
        scratch_shapes=[pltpu.SMEM((2, 1024 + 128), jnp.int32)],
        compiler_params=pltpu.CompilerParams(vmem_limit_bytes=20 * 2**20),
        name="tiles",
    )(lists, counts, split)
    summed = pl.pallas_call(
        scatter_kernel,
        out_shape=jax.ShapeDtypeStruct((8, TR, TR), F32),
        in_specs=[vmem],
        out_specs=vmem,
        scratch_shapes=[
            pltpu.VMEM((2, 2, 8, TR, TR), F32),
            pltpu.VMEM((2, 2, 16, TR, TR), F32),
            pltpu.VMEM((2, 2, 8, TR, TR), F32),
            pltpu.VMEM((2, 16, TR, TR), F32),
            pltpu.VMEM((2, 2, 2, TR, TR), F32),
            pltpu.VMEM((2, 2, 4, TR, TR), F32),
            pltpu.VMEM((2, 2, 2, TR, TR), F32),
            dma((24,)),
            dma((24,)),
        ],
        compiler_params=pltpu.CompilerParams(collective_id=1, has_side_effects=True, vmem_limit_bytes=20 * 2**20),
        name="scatter",
    )(part)
    return parent_entries - summed


def solution(mesh):
    in_specs = (P("front", "blk", None), P("front"), P(), P(), P(("front", "blk"), None, None))
    out_specs = P(("front", "blk"), None, None)
    return jax.shard_map(
        per_device, mesh=mesh, in_specs=in_specs, out_specs=out_specs, check_vma=False
    )
```

```python
import functools

import jax
import jax.numpy as jnp
from jax import lax
from jax.experimental import pallas as pl
from jax.experimental.pallas import tpu as pltpu
from jax.sharding import PartitionSpec as P

TR = 128
KH = 512
CB = 4
EB = 32
UNROLL = 8
BATCH = 16
FIXED = 32
REST = 256
TRASH = 128

MESH = pl.DeviceIdType.MESH
F32 = jnp.float32
BF16 = jnp.bfloat16


def position():
    front, blk = lax.axis_index("front"), lax.axis_index("blk")
    return dict(
        front=front,
        blk=blk,
        y=front // 4,
        xl=(front // 2) % 2,
        core=front % 2,
        xh=blk // 4,
        z=blk % 4,
    )


def device(p, **moves):
    q = {**p, **moves}
    return {"front": q["y"] * 4 + q["xl"] * 2 + q["core"], "blk": q["xh"] * 4 + q["z"]}


def slot(xs, dz, c):
    return (xs * 4 + dz) * CB + c


def gather_kernel(
    x, parents, sizes, counts, split, staged, codes, rest, totals,
    mine, other, fs, fs_other, targets, size_s, count_s, code_s, rows_by_place,
    x_send, z_send, recv, core_send, core_recv, local, fs_sem,
):
    p = position()
    z, xh = p["z"], p["xh"]
    up, down = device(p, z=(z + 1) % 4), device(p, z=(z + 3) % 4)
    across = device(p, xh=1 - xh)
    twin = device(p, core=1 - p["core"])

    fronts = [(p["front"] // 2) * 2 + (p["core"] if g == 0 else 1 - p["core"]) for g in range(2)]
    small = [
        pltpu.make_async_copy(sizes, size_s, local.at[4]),
        pltpu.make_async_copy(counts, count_s, local.at[5]),
        pltpu.make_async_copy(parents.at[fronts[0]], targets.at[0], local.at[6]),
        pltpu.make_async_copy(parents.at[fronts[1]], targets.at[1], local.at[7]),
    ]
    for copy in small:
        copy.start()
    barrier = pltpu.get_barrier_semaphore()
    for other_dev in (up, down, across, twin):
        pl.semaphore_signal(barrier, inc=1, device_id=other_dev, device_id_type=MESH)
    pl.semaphore_wait(barrier, 4)

    sent = []

    def send(src, dst, ssem, rsem, to):
        copy = pltpu.make_async_remote_copy(
            src_ref=src, dst_ref=dst, send_sem=ssem, recv_sem=rsem, device_id=to, device_id_type=MESH
        )
        copy.start()
        sent.append(copy)

    n_z = [0]

    def send_z(src, xs, dz, c, to):
        s = slot(xs, dz, c)
        send(src, mine.at[s], z_send.at[n_z[0]], recv.at[s], to)
        n_z[0] += 1

    def arrived(s):
        pltpu.make_async_remote_copy(
            src_ref=mine.at[s], dst_ref=mine.at[s], send_sem=z_send.at[0], recv_sem=recv.at[s],
            device_id=up, device_id_type=MESH,
        ).wait_recv()

    def to_twin(s):
        send(mine.at[s], other.at[s], core_send.at[s], core_recv.at[s], twin)

    def from_twin(s):
        pltpu.make_async_remote_copy(
            src_ref=mine.at[s], dst_ref=other.at[s], send_sem=core_send.at[s], recv_sem=core_recv.at[s],
            device_id=twin, device_id_type=MESH,
        ).wait_recv()

    own_cols = pl.ds(pl.multiple_of(xh * KH, KH), KH)
    across_cols = pl.ds(pl.multiple_of((1 - xh) * KH, KH), KH)

    def rows(c):
        return pl.ds(c * TR, TR)

    small[0].wait()
    fs[...] = jnp.full((8, KH), size_s[0], jnp.int32)
    loads = []
    for c in (0, 2, 1, 3):
        s = slot(1, 0, c)
        send(x.at[rows(c), across_cols], mine.at[s], x_send.at[c], recv.at[s], across)
    for c, d in ((0, 2), (1, 3), (2, 0), (3, 1)):
        send_z(x.at[rows(c), own_cols], 0, 3, c, up)
        send_z(x.at[rows(d), own_cols], 0, 1, d, down)
        load = pltpu.make_async_copy(x.at[rows(c), own_cols], mine.at[slot(0, 0, c)], local.at[c])
        load.start()
        loads.append(load)

    for copy in small[1:]:
        copy.wait()
    send(fs, fs_other, fs_sem.at[0], fs_sem.at[1], twin)
    fs_copy = sent[-1]

    col = lax.broadcasted_iota(jnp.int32, (EB, EB), 1)
    row = lax.broadcasted_iota(jnp.int32, (EB, EB), 0)
    lower = (row >= col).astype(F32)
    before = (row < col).astype(F32)

    def place_of(block):
        return ((((block >> 4) ^ xh) << 4) + ((((block >> 2) - z) & 3) << 2)) + (block & 3)

    def level_of(s):
        return jnp.where(s < 20, 0, jnp.where((s >= 24) & (s < 28), 2, 1))

    a_slot, b_slot = place_of(row), place_of(col)
    level = jnp.maximum(level_of(a_slot), level_of(b_slot))

    def places(hit):
        rank = jnp.dot(lower, hit.astype(F32), preferred_element_type=F32)
        many = jnp.broadcast_to(rank[EB - 1 : EB, :], (8, EB))
        start = jnp.dot(many, before, preferred_element_type=F32)
        at = (rank + start[0:1, :]).astype(jnp.int32) - 1
        return jnp.where(hit, at, -1), jnp.sum(many[0:1, :], axis=1, keepdims=True).astype(jnp.int32)

    ones = jnp.full((8, EB), 1.0, F32)

    def listed(at, code, size):
        def eight(i, _):
            first = pl.multiple_of(i * 8, 8)
            for k in range(8):
                rows_by_place[pl.ds(first + k, 1), 0:EB] = jnp.sum(
                    jnp.where(at == first + k, code, 0.0), axis=0, keepdims=True
                )
            return 0

        lax.fori_loop(0, size // 8, eight, 0)
        found = lax.dot_general(
            ones, rows_by_place[0:size, 0:EB], (((1,), (1,)), ((), ())),
            precision=lax.Precision.HIGHEST, preferred_element_type=F32,
        )
        return found[0:1, :].astype(jnp.int32)

    def plan(g):
        target = targets[g]
        live = count_s[fronts[g]]
        dest = target >> 3
        dest_front, dest_blk = dest >> 3, dest & 7
        hit = ((dest_blk & 3) == z) & ((dest_front & 1) == p["core"])
        hit = hit & (row < live) & (col < live)
        rx = ((dest_blk >> 2) * 2 + ((dest_front >> 1) & 1) - (p["xh"] * 2 + p["xl"])) & 3
        ry = ((dest_front >> 2) - p["y"]) & 3
        place = target & 7
        first = place < 4
        at = jnp.where(first, ry * 4 + rx, 16 + rx * 4 + ry) * 4 + (place & 3)
        code = ((b_slot << 13) + (a_slot << 8) + at).astype(F32)
        over = level == 2
        for n in range(2):
            where, many = places(hit & (level == n))
            codes[g * 2 + n : g * 2 + n + 1, 0:FIXED] = listed(where, code, FIXED)
            totals[g * 2 + n : g * 2 + n + 1, :] = jnp.broadcast_to(many, (1, 128))
            over = over | (where >= FIXED)
        where, many = places(hit & over)
        rest[g : g + 1, :] = listed(where, code, REST)
        totals[4 + g : 5 + g, :] = jnp.broadcast_to(many, (1, 128))

    def products(g, n, first, steps):
        def step(i, _):
            for u in range(BATCH):
                t = (first + i) * BATCH + u
                c = code_s[g * 2 + n, t]
                d = lax.dot_general(
                    split[g, (c >> 8) & 31], split[g, (c >> 13) & 31], (((1,), (1,)), ((), ())),
                    preferred_element_type=F32,
                )
                staged[g, n * FIXED + t] = d[:TR, :TR] + (d[:TR, TR:] + d[TR:, :TR])
            return 0

        lax.fori_loop(0, steps, step, 0)

    def convert(g, s):
        src = mine if g == 0 else other
        size = (fs if g == 0 else fs_other)[0:1, :]
        block = lax.broadcasted_iota(jnp.int32, (1, KH), 1) // TR + xh * (KH // TR)
        keep = block < size

        def step(i, _):
            at = pl.multiple_of(i * 16, 16)
            v = jnp.where(keep, src[s, pl.ds(at, 16), :], 0.0)
            hi = v.astype(BF16)
            split[g, s, pl.ds(at, 16), :] = hi
            split[g, s, pl.ds(TR + at, 16), :] = (v - hi.astype(F32)).astype(BF16)
            return 0

        lax.fori_loop(0, TR // 16, step, 0)

    twin_queue = []

    def take(s):
        to_twin(s)
        convert(0, s)
        twin_queue.append(s)
        if len(twin_queue) > 4:
            drain()

    def drain():
        t = twin_queue.pop(0)
        from_twin(t)
        convert(1, t)

    plan(0)
    fs_copy.wait_recv()
    for c, load in zip((0, 1, 2, 3), loads):
        load.wait()
        take(slot(0, 0, c))
    for i in range(4):
        c, d = (0, 1, 2, 3)[i], (2, 3, 0, 1)[i]
        arrived(slot(0, 3, c))
        if c < 2:
            send_z(mine.at[slot(0, 3, c)], 0, 2, c, up)
        take(slot(0, 3, c))
        arrived(slot(0, 1, d))
        if d >= 2:
            send_z(mine.at[slot(0, 1, d)], 0, 2, d, down)
        take(slot(0, 1, d))
        e = (0, 2, 1, 3)[i]
        s = slot(1, 0, e)
        arrived(s)
        send_z(mine.at[s], 1, 3, e, up)
        send_z(mine.at[s], 1, 1, e, down)
        take(s)
        if i == 0:
            plan(1)
        if i == 2:
            code_copy = pltpu.make_async_copy(codes, code_s, local.at[8])
            code_copy.start()
    for e in (0, 2, 1, 3):
        arrived(slot(0, 2, e))
        take(slot(0, 2, e))
    code_copy.wait()
    while twin_queue:
        drain()
    work = [(0, 0), (1, 0), (0, 1), (1, 1)]
    for e, many in zip((0, 2, 1, 3), (1, 1, 1, 1)):
        s = slot(1, 3, e)
        arrived(s)
        if e < 2:
            send_z(mine.at[s], 1, 2, e, up)
        take(s)
        s = slot(1, 1, e)
        arrived(s)
        if e >= 2:
            send_z(mine.at[s], 1, 2, e, down)
        take(s)
        for _ in range(many):
            g, first = work.pop(0)
            products(g, 0, first, 1)
    while twin_queue:
        drain()
    products(0, 1, 0, 2)
    for e in (0, 2):
        arrived(slot(1, 2, e))
        take(slot(1, 2, e))
    products(1, 1, 0, 2)
    for e in (1, 3):
        arrived(slot(1, 2, e))
        take(slot(1, 2, e))
    while twin_queue:
        drain()
    for copy in sent:
        copy.wait_send()


def tiles_kernel(codes, rest, totals, held, staged, acc, flat):
    def clear(i, _):
        acc[i] = jnp.zeros((TR, TR), F32)
        return 0

    lax.fori_loop(0, TRASH + 1, clear, 0)
    for g in range(2):
        for n in range(2):
            many = totals[g * 2 + n, 0]

            def add(i, _):
                for u in range(8):
                    t = i * 8 + u
                    at = jnp.where(t < many, codes[g * 2 + n, t] & 255, TRASH)
                    acc[at] += staged[g, n * FIXED + t]
                return 0

            lax.fori_loop(0, FIXED // 8, add, 0)
    count = 0
    for g in range(2):
        def entry(k, _):
            flat[count + k] = rest[g, k] + (g << 18)
            return 0

        lax.fori_loop(0, totals[4 + g, 0], entry, 0)
        count = count + totals[4 + g, 0]
    for u in range(UNROLL - 1):
        flat[count + u] = TRASH

    def several(i, _):
        for u in range(UNROLL):
            c = flat[i * UNROLL + u]
            g, b, a, at = c >> 18, (c >> 13) & 31, (c >> 8) & 31, c & 255
            d = lax.dot_general(
                held[g, a], held[g, b], (((1,), (1,)), ((), ())), preferred_element_type=F32
            )
            acc[at] += d[:TR, :TR] + (d[:TR, TR:] + d[TR:, :TR])
        return 0

    lax.fori_loop(0, (count + UNROLL - 1) // UNROLL, several, 0)


def scatter_kernel(
    part, out, opp, near, fwd, mid, mid_opp, mid_near, mid_fwd,
    send_sem, recv_sem,
):
    p = position()
    x = p["xh"] * 2 + p["xl"]

    def along_x(d):
        n = (x + d) % 4
        return device(p, xh=n // 2, xl=n % 2)

    def along_y(d):
        return device(p, y=(p["y"] + d) % 4)

    barrier = pltpu.get_barrier_semaphore()
    for to in (along_x(1), along_x(3), along_y(1), along_y(3)):
        pl.semaphore_signal(barrier, inc=1, device_id=to, device_id_type=MESH)
    pl.semaphore_wait(barrier, 4)

    sent = []
    count = [0]

    def send(src, dst, to):
        k = count[0]
        count[0] += 1
        copy = pltpu.make_async_remote_copy(
            src_ref=src, dst_ref=dst, send_sem=send_sem.at[k], recv_sem=recv_sem.at[k],
            device_id=to, device_id_type=MESH,
        )
        copy.start()
        sent.append(copy)
        return copy

    def begin(src, n, h, to, opp, near):
        half = n // 2
        o_up = send(src(2, 0, half), opp.at[h, 0], to(1))
        o_down = send(src(2, half, half), opp.at[h, 1], to(3))
        n_up = send(src(1, half, half), near.at[h, 0, pl.ds(half, half)], to(1))
        n_down = send(src(3, 0, half), near.at[h, 1, pl.ds(0, half)], to(3))
        return o_up, o_down, n_up, n_down

    def relay(copies, val, n, h, to, opp, near, fwd):
        half = n // 2
        copies[0].wait_recv()
        fwd[h, 0] = val(1, 0, half) + opp[h, 0]
        f_up = send(fwd.at[h, 0], near.at[h, 0, pl.ds(0, half)], to(1))
        copies[1].wait_recv()
        fwd[h, 1] = val(3, half, half) + opp[h, 1]
        f_down = send(fwd.at[h, 1], near.at[h, 1, pl.ds(half, half)], to(3))
        return copies[2], copies[3], f_up, f_down

    ways = ((along_y, along_x), (along_x, along_y))
    firsts = []
    for h in range(2):
        firsts.append(
            begin(lambda r, lo, size: part.at[pl.ds(h * 64 + r * 16 + lo, size)], 16, h, ways[h][0], opp, near)
        )
    seconds = []
    for h in range(2):
        firsts[h] = relay(
            firsts[h], lambda r, lo, size: part[pl.ds(h * 64 + r * 16 + lo, size)], 16, h, ways[h][0], opp, near, fwd
        )
    for h in range(2):
        for copy in firsts[h]:
            copy.wait_recv()
        mid[h] = part[pl.ds(h * 64, 16)] + (near[h, 0] + near[h, 1])
        seconds.append(
            begin(lambda r, lo, size: mid.at[h, pl.ds(r * 4 + lo, size)], 4, h, ways[h][1], mid_opp, mid_near)
        )
    for h in range(2):
        seconds[h] = relay(
            seconds[h], lambda r, lo, size: mid[h, pl.ds(r * 4 + lo, size)], 4, h, ways[h][1], mid_opp, mid_near, mid_fwd
        )
    for h in range(2):
        for copy in seconds[h]:
            copy.wait_recv()
        out[pl.ds(h * 4, 4)] = mid[h, pl.ds(0, 4)] + (mid_near[h, 0] + mid_near[h, 1])
    for copy in sent:
        copy.wait_send()


def per_device(factor_rows, front_sizes, tile_counts, parent_tiles, parent_entries):
    vmem = pl.BlockSpec(memory_space=pltpu.VMEM)
    smem = pl.BlockSpec(memory_space=pltpu.SMEM)
    dma = pltpu.SemaphoreType.DMA
    hbm = pl.BlockSpec(memory_space=pltpu.HBM)
    split, staged, codes, rest, totals = pl.pallas_call(
        gather_kernel,
        out_shape=(
            jax.ShapeDtypeStruct((2, EB, 2 * TR, KH), BF16),
            jax.ShapeDtypeStruct((2, 2 * FIXED, TR, TR), F32),
            jax.ShapeDtypeStruct((8, 128), jnp.int32),
            jax.ShapeDtypeStruct((8, REST), jnp.int32),
            jax.ShapeDtypeStruct((8, 128), jnp.int32),
        ),
        in_specs=[hbm, hbm, hbm, hbm],
        out_specs=(vmem, vmem, vmem, vmem, vmem),
        scratch_shapes=[
            pltpu.VMEM((EB, TR, KH), F32),
            pltpu.VMEM((EB, TR, KH), F32),
            pltpu.VMEM((8, KH), jnp.int32),
            pltpu.VMEM((8, KH), jnp.int32),
            pltpu.VMEM((2, EB, EB), jnp.int32),
            pltpu.SMEM((1,), jnp.int32),
            pltpu.SMEM((16,), jnp.int32),
            pltpu.SMEM((8, 128), jnp.int32),
            pltpu.VMEM((REST, 128), F32),
            dma((4,)),
            dma((24,)),
            dma((32,)),
            dma((32,)),
            dma((32,)),
            dma((9,)),
            dma((2,)),
        ],
        compiler_params=pltpu.CompilerParams(collective_id=0, has_side_effects=True, vmem_limit_bytes=18 * 2**20),
        name="gather",
    )(factor_rows[0], parent_tiles, front_sizes, tile_counts)
    part = pl.pallas_call(
        tiles_kernel,
        out_shape=jax.ShapeDtypeStruct((TRASH + 1, TR, TR), F32),
        in_specs=[smem, smem, smem, vmem, vmem],
        out_specs=vmem,
        scratch_shapes=[pltpu.SMEM((2 * REST + UNROLL,), jnp.int32)],
        compiler_params=pltpu.CompilerParams(vmem_limit_bytes=4 * 2**20),
        name="tiles",
    )(codes, rest, totals, split, staged)
    summed = pl.pallas_call(
        scatter_kernel,
        out_shape=jax.ShapeDtypeStruct((8, TR, TR), F32),
        in_specs=[vmem],
        out_specs=vmem,
        scratch_shapes=[
            pltpu.VMEM((2, 2, 8, TR, TR), F32),
            pltpu.VMEM((2, 2, 16, TR, TR), F32),
            pltpu.VMEM((2, 2, 8, TR, TR), F32),
            pltpu.VMEM((2, 16, TR, TR), F32),
            pltpu.VMEM((2, 2, 2, TR, TR), F32),
            pltpu.VMEM((2, 2, 4, TR, TR), F32),
            pltpu.VMEM((2, 2, 2, TR, TR), F32),
            dma((24,)),
            dma((24,)),
        ],
        compiler_params=pltpu.CompilerParams(collective_id=1, has_side_effects=True, vmem_limit_bytes=14 * 2**20),
        name="scatter",
    )(part)
    return parent_entries - summed


def solution(mesh):
    in_specs = (P("front", "blk", None), P("front"), P(), P(), P(("front", "blk"), None, None))
    out_specs = P(("front", "blk"), None, None)
    return jax.shard_map(
        per_device, mesh=mesh, in_specs=in_specs, out_specs=out_specs, check_vma=False
    )
```

```python
import functools

import jax
import jax.numpy as jnp
from jax import lax
from jax.experimental import pallas as pl
from jax.experimental.pallas import tpu as pltpu
from jax.sharding import PartitionSpec as P

TR = 128
KH = 512
CB = 4
EB = 32
UNROLL = 8
BATCH = 16
FIXED = (48, 48, 16)
REUSED = 40
FREED = (20, 21, 22, 23, 28, 29, 30, 31)
REST = 256
TRASH = 128

MESH = pl.DeviceIdType.MESH
F32 = jnp.float32
BF16 = jnp.bfloat16


def position():
    front, blk = lax.axis_index("front"), lax.axis_index("blk")
    return dict(
        front=front,
        blk=blk,
        y=front // 4,
        xl=(front // 2) % 2,
        core=front % 2,
        xh=blk // 4,
        z=blk % 4,
    )


def device(p, **moves):
    q = {**p, **moves}
    return {"front": q["y"] * 4 + q["xl"] * 2 + q["core"], "blk": q["xh"] * 4 + q["z"]}


def slot(xs, dz, c):
    return (xs * 4 + dz) * CB + c


def gather_kernel(
    x, parents, sizes, counts, split, other, staged, codes, rest, totals,
    mine, fs, fs_other, targets, count_s, code_s, rows_by_place,
    x_send, z_send, recv, core_send, core_recv, local, fs_sem,
):
    p = position()
    z, xh = p["z"], p["xh"]
    up, down = device(p, z=(z + 1) % 4), device(p, z=(z + 3) % 4)
    across = device(p, xh=1 - xh)
    twin = device(p, core=1 - p["core"])

    fronts = [(p["front"] // 2) * 2 + (p["core"] if g == 0 else 1 - p["core"]) for g in range(2)]
    small = [
        pltpu.make_async_copy(counts, count_s, local.at[5]),
        pltpu.make_async_copy(parents.at[fronts[0]], targets.at[0], local.at[6]),
        pltpu.make_async_copy(parents.at[fronts[1]], targets.at[1], local.at[7]),
    ]
    for copy in small:
        copy.start()
    barrier = pltpu.get_barrier_semaphore()
    for other_dev in (up, down, across, twin):
        pl.semaphore_signal(barrier, inc=1, device_id=other_dev, device_id_type=MESH)
    pl.semaphore_wait(barrier, 4)

    sent = []

    def send(src, dst, ssem, rsem, to):
        copy = pltpu.make_async_remote_copy(
            src_ref=src, dst_ref=dst, send_sem=ssem, recv_sem=rsem, device_id=to, device_id_type=MESH
        )
        copy.start()
        sent.append(copy)

    n_z = [0]

    def send_z(src, xs, dz, c, to):
        s = slot(xs, dz, c)
        send(src, mine.at[s], z_send.at[n_z[0]], recv.at[s], to)
        n_z[0] += 1

    def arrived(s):
        pltpu.make_async_remote_copy(
            src_ref=mine.at[s], dst_ref=mine.at[s], send_sem=z_send.at[0], recv_sem=recv.at[s],
            device_id=up, device_id_type=MESH,
        ).wait_recv()

    def to_twin(s):
        send(mine.at[s], other.at[s], core_send.at[s], core_recv.at[s], twin)

    def from_twin(s):
        pltpu.make_async_remote_copy(
            src_ref=mine.at[s], dst_ref=other.at[s], send_sem=core_send.at[s], recv_sem=core_recv.at[s],
            device_id=twin, device_id_type=MESH,
        ).wait_recv()

    own_cols = pl.ds(pl.multiple_of(xh * KH, KH), KH)
    across_cols = pl.ds(pl.multiple_of((1 - xh) * KH, KH), KH)

    def rows(c):
        return pl.ds(c * TR, TR)

    fs[...] = jnp.full((8, KH), sizes[0], jnp.int32)
    loads = []
    for c in (0, 2, 1, 3):
        s = slot(1, 0, c)
        send(x.at[rows(c), across_cols], mine.at[s], x_send.at[c], recv.at[s], across)
    for c, d in ((0, 2), (1, 3), (2, 0), (3, 1)):
        send_z(x.at[rows(c), own_cols], 0, 3, c, up)
        send_z(x.at[rows(d), own_cols], 0, 1, d, down)
        load = pltpu.make_async_copy(x.at[rows(c), own_cols], mine.at[slot(0, 0, c)], local.at[c])
        load.start()
        loads.append(load)

    for copy in small:
        copy.wait()
    send(fs, fs_other, fs_sem.at[0], fs_sem.at[1], twin)
    fs_copy = sent[-1]

    col = lax.broadcasted_iota(jnp.int32, (EB, EB), 1)
    row = lax.broadcasted_iota(jnp.int32, (EB, EB), 0)
    lower = (row >= col).astype(F32)
    before = (row < col).astype(F32)

    def place_of(block):
        return ((((block >> 4) ^ xh) << 4) + ((((block >> 2) - z) & 3) << 2)) + (block & 3)

    def level_of(s):
        return jnp.where(s < 20, 0, jnp.where((s >= 24) & (s < 28), 2 + (s & 1), 1))

    a_slot, b_slot = place_of(row), place_of(col)
    level = jnp.maximum(level_of(a_slot), level_of(b_slot))

    def places(hit):
        rank = jnp.dot(lower, hit.astype(F32), preferred_element_type=F32)
        many = jnp.broadcast_to(rank[EB - 1 : EB, :], (8, EB))
        start = jnp.dot(many, before, preferred_element_type=F32)
        at = (rank + start[0:1, :]).astype(jnp.int32) - 1
        return jnp.where(hit, at, -1), jnp.sum(many[0:1, :], axis=1, keepdims=True).astype(jnp.int32)

    ones = jnp.full((8, EB), 1.0, F32)

    def listed(at, code, size):
        def eight(i, _):
            first = pl.multiple_of(i * 8, 8)
            for k in range(8):
                rows_by_place[pl.ds(first + k, 1), 0:EB] = jnp.sum(
                    jnp.where(at == first + k, code, 0.0), axis=0, keepdims=True
                )
            return 0

        lax.fori_loop(0, size // 8, eight, 0)
        found = lax.dot_general(
            ones, rows_by_place[0:size, 0:EB], (((1,), (1,)), ((), ())),
            precision=lax.Precision.HIGHEST, preferred_element_type=F32,
        )
        return found[0:1, :].astype(jnp.int32)

    def plan(g):
        target = targets[g]
        live = count_s[fronts[g]]
        dest = target >> 3
        dest_front, dest_blk = dest >> 3, dest & 7
        hit = ((dest_blk & 3) == z) & ((dest_front & 1) == p["core"])
        hit = hit & (row < live) & (col < live)
        rx = ((dest_blk >> 2) * 2 + ((dest_front >> 1) & 1) - (p["xh"] * 2 + p["xl"])) & 3
        ry = ((dest_front >> 2) - p["y"]) & 3
        place = target & 7
        first = place < 4
        at = jnp.where(first, ry * 4 + rx, 16 + rx * 4 + ry) * 4 + (place & 3)
        code = ((b_slot << 13) + (a_slot << 8) + at).astype(F32)
        over = level == 3
        for n in range(3):
            where, many = places(hit & (level == n))
            codes[g * 4 + n : g * 4 + n + 1, 0 : FIXED[n]] = listed(where, code, FIXED[n])
            totals[g * 4 + n : g * 4 + n + 1, :] = jnp.broadcast_to(many, (1, 128))
            over = over | (where >= FIXED[n])
        where, many = places(hit & over)
        rest[g : g + 1, :] = listed(where, code, REST)
        totals[g * 4 + 3 : g * 4 + 4, :] = jnp.broadcast_to(many, (1, 128))

    def product(g, n, t):
        c = code_s[g * 4 + n, t]
        d = lax.dot_general(
            split[g, (c >> 8) & 31], split[g, (c >> 13) & 31], (((1,), (1,)), ((), ())),
            preferred_element_type=F32,
        )
        return d[:TR, :TR] + (d[:TR, TR:] + d[TR:, :TR])

    def products(g, n, first):
        for t in range(first * BATCH, (first + 1) * BATCH):
            lanes = pl.ds((t % 4) * TR, TR)
            if n == 2:
                other[FREED[g * 4 + t // 4], :, lanes] = product(g, n, t)
            elif t < REUSED:
                other[g * 10 + t // 4, :, lanes] = product(g, n, t)
            else:
                staged[g, t - REUSED] = product(g, n, t)

    def products_1(g):
        def step(i, _):
            for u in range(BATCH):
                t = i * BATCH + u
                staged[g, FIXED[0] - REUSED + t] = product(g, 1, t)
            return 0

        lax.fori_loop(0, FIXED[1] // BATCH, step, 0)

    def convert(g, s):
        src = mine if g == 0 else other
        size = (fs if g == 0 else fs_other)[0:1, :]
        block = lax.broadcasted_iota(jnp.int32, (1, KH), 1) // TR + xh * (KH // TR)
        keep = block < size

        def step(i, _):
            at = pl.multiple_of(i * 16, 16)
            v = jnp.where(keep, src[s, pl.ds(at, 16), :], 0.0)
            hi = v.astype(BF16)
            split[g, s, pl.ds(at, 16), :] = hi
            split[g, s, pl.ds(TR + at, 16), :] = (v - hi.astype(F32)).astype(BF16)
            return 0

        lax.fori_loop(0, TR // 16, step, 0)

    twin_queue = []

    def take(s):
        to_twin(s)
        convert(0, s)
        twin_queue.append(s)
        if len(twin_queue) > 4:
            drain()

    def drain():
        t = twin_queue.pop(0)
        from_twin(t)
        convert(1, t)

    plan(0)
    fs_copy.wait_recv()
    for c, load in zip((0, 1, 2, 3), loads):
        load.wait()
        take(slot(0, 0, c))
    for i in range(4):
        c, d = (0, 1, 2, 3)[i], (2, 3, 0, 1)[i]
        arrived(slot(0, 3, c))
        if c < 2:
            send_z(mine.at[slot(0, 3, c)], 0, 2, c, up)
        take(slot(0, 3, c))
        arrived(slot(0, 1, d))
        if d >= 2:
            send_z(mine.at[slot(0, 1, d)], 0, 2, d, down)
        take(slot(0, 1, d))
        e = (0, 2, 1, 3)[i]
        s = slot(1, 0, e)
        arrived(s)
        send_z(mine.at[s], 1, 3, e, up)
        send_z(mine.at[s], 1, 1, e, down)
        take(s)
        if i == 0:
            plan(1)
        if i == 2:
            code_copy = pltpu.make_async_copy(codes, code_s, local.at[8])
            code_copy.start()
    for e in (0, 2, 1, 3):
        arrived(slot(0, 2, e))
        take(slot(0, 2, e))
    code_copy.wait()
    while twin_queue:
        drain()
    work = [(0, 0), (1, 0), (0, 1), (1, 1), (0, 2), (1, 2)]
    for e, many in zip((0, 2, 1, 3), (2, 2, 1, 1)):
        s = slot(1, 3, e)
        arrived(s)
        if e < 2:
            send_z(mine.at[s], 1, 2, e, up)
        take(s)
        s = slot(1, 1, e)
        arrived(s)
        if e >= 2:
            send_z(mine.at[s], 1, 2, e, down)
        take(s)
        for _ in range(many):
            g, first = work.pop(0)
            products(g, 0, first)
    while twin_queue:
        drain()
    products_1(0)
    for e in (0, 2):
        arrived(slot(1, 2, e))
        take(slot(1, 2, e))
    products_1(1)
    while twin_queue:
        drain()
    products(0, 2, 0)
    for e in (1, 3):
        arrived(slot(1, 2, e))
        take(slot(1, 2, e))
    products(1, 2, 0)
    while twin_queue:
        drain()
    for copy in sent:
        copy.wait_send()


def tiles_kernel(codes, rest, totals, held, reused, staged, acc, flat):
    def clear(i, _):
        acc[i] = jnp.zeros((TR, TR), F32)
        return 0

    lax.fori_loop(0, TRASH + 1, clear, 0)
    def add(g, n, t, value):
        at = jnp.where(t < totals[g * 4 + n, 0], codes[g * 4 + n, t] & 255, TRASH)
        acc[at] += value

    for g in range(2):
        def four(i, _):
            for u in range(4):
                add(g, 0, i * 4 + u, reused[g * 10 + i, :, pl.ds(u * TR, TR)])
            return 0

        lax.fori_loop(0, REUSED // 4, four, 0)
        for t in range(REUSED, FIXED[0]):
            add(g, 0, t, staged[g, t - REUSED])

        def eight(i, _):
            for u in range(8):
                add(g, 1, i * 8 + u, staged[g, FIXED[0] - REUSED + i * 8 + u])
            return 0

        lax.fori_loop(0, FIXED[1] // 8, eight, 0)
        for t in range(FIXED[2]):
            add(g, 2, t, reused[FREED[g * 4 + t // 4], :, pl.ds((t % 4) * TR, TR)])
    count = 0
    for g in range(2):
        def entry(k, _):
            flat[count + k] = rest[g, k] + (g << 18)
            return 0

        lax.fori_loop(0, totals[g * 4 + 3, 0], entry, 0)
        count = count + totals[g * 4 + 3, 0]
    for u in range(UNROLL - 1):
        flat[count + u] = TRASH

    def several(i, _):
        for u in range(UNROLL):
            c = flat[i * UNROLL + u]
            g, b, a, at = c >> 18, (c >> 13) & 31, (c >> 8) & 31, c & 255
            d = lax.dot_general(
                held[g, a], held[g, b], (((1,), (1,)), ((), ())), preferred_element_type=F32
            )
            acc[at] += d[:TR, :TR] + (d[:TR, TR:] + d[TR:, :TR])
        return 0

    lax.fori_loop(0, (count + UNROLL - 1) // UNROLL, several, 0)


def scatter_kernel(
    part, out, opp, near, fwd, mid, mid_opp, mid_near, mid_fwd,
    send_sem, recv_sem,
):
    p = position()
    x = p["xh"] * 2 + p["xl"]

    def along_x(d):
        n = (x + d) % 4
        return device(p, xh=n // 2, xl=n % 2)

    def along_y(d):
        return device(p, y=(p["y"] + d) % 4)

    barrier = pltpu.get_barrier_semaphore()
    for to in (along_x(1), along_x(3), along_y(1), along_y(3)):
        pl.semaphore_signal(barrier, inc=1, device_id=to, device_id_type=MESH)
    pl.semaphore_wait(barrier, 4)

    sent = []
    count = [0]

    def send(src, dst, to):
        k = count[0]
        count[0] += 1
        copy = pltpu.make_async_remote_copy(
            src_ref=src, dst_ref=dst, send_sem=send_sem.at[k], recv_sem=recv_sem.at[k],
            device_id=to, device_id_type=MESH,
        )
        copy.start()
        sent.append(copy)
        return copy

    def begin(src, n, h, to, opp, near):
        half = n // 2
        o_up = send(src(2, 0, half), opp.at[h, 0], to(1))
        o_down = send(src(2, half, half), opp.at[h, 1], to(3))
        n_up = send(src(1, half, half), near.at[h, 0, pl.ds(half, half)], to(1))
        n_down = send(src(3, 0, half), near.at[h, 1, pl.ds(0, half)], to(3))
        return o_up, o_down, n_up, n_down

    def relay(copies, val, n, h, to, opp, near, fwd):
        half = n // 2
        copies[0].wait_recv()
        fwd[h, 0] = val(1, 0, half) + opp[h, 0]
        f_up = send(fwd.at[h, 0], near.at[h, 0, pl.ds(0, half)], to(1))
        copies[1].wait_recv()
        fwd[h, 1] = val(3, half, half) + opp[h, 1]
        f_down = send(fwd.at[h, 1], near.at[h, 1, pl.ds(half, half)], to(3))
        return copies[2], copies[3], f_up, f_down

    ways = ((along_y, along_x), (along_x, along_y))
    firsts = []
    for h in range(2):
        firsts.append(
            begin(lambda r, lo, size: part.at[pl.ds(h * 64 + r * 16 + lo, size)], 16, h, ways[h][0], opp, near)
        )
    seconds = []
    for h in range(2):
        firsts[h] = relay(
            firsts[h], lambda r, lo, size: part[pl.ds(h * 64 + r * 16 + lo, size)], 16, h, ways[h][0], opp, near, fwd
        )
    for h in range(2):
        for copy in firsts[h]:
            copy.wait_recv()
        mid[h] = part[pl.ds(h * 64, 16)] + (near[h, 0] + near[h, 1])
        seconds.append(
            begin(lambda r, lo, size: mid.at[h, pl.ds(r * 4 + lo, size)], 4, h, ways[h][1], mid_opp, mid_near)
        )
    for h in range(2):
        seconds[h] = relay(
            seconds[h], lambda r, lo, size: mid[h, pl.ds(r * 4 + lo, size)], 4, h, ways[h][1], mid_opp, mid_near, mid_fwd
        )
    for h in range(2):
        for copy in seconds[h]:
            copy.wait_recv()
        out[pl.ds(h * 4, 4)] = mid[h, pl.ds(0, 4)] + (mid_near[h, 0] + mid_near[h, 1])
    for copy in sent:
        copy.wait_send()


def per_device(factor_rows, front_sizes, tile_counts, parent_tiles, parent_entries):
    vmem = pl.BlockSpec(memory_space=pltpu.VMEM)
    smem = pl.BlockSpec(memory_space=pltpu.SMEM)
    dma = pltpu.SemaphoreType.DMA
    hbm = pl.BlockSpec(memory_space=pltpu.HBM)

    def in_hbm(a):
        return pltpu.with_memory_space_constraint(a, pltpu.HBM)

    split, reused, staged, codes, rest, totals = pl.pallas_call(
        gather_kernel,
        out_shape=(
            jax.ShapeDtypeStruct((2, EB, 2 * TR, KH), BF16),
            jax.ShapeDtypeStruct((EB, TR, KH), F32),
            jax.ShapeDtypeStruct((2, FIXED[0] - REUSED + FIXED[1], TR, TR), F32),
            jax.ShapeDtypeStruct((8, 128), jnp.int32),
            jax.ShapeDtypeStruct((8, REST), jnp.int32),
            jax.ShapeDtypeStruct((8, 128), jnp.int32),
        ),
        in_specs=[hbm, hbm, smem, hbm],
        out_specs=(vmem,) * 6,
        scratch_shapes=[
            pltpu.VMEM((EB, TR, KH), F32),
            pltpu.VMEM((8, KH), jnp.int32),
            pltpu.VMEM((8, KH), jnp.int32),
            pltpu.VMEM((2, EB, EB), jnp.int32),
            pltpu.SMEM((16,), jnp.int32),
            pltpu.SMEM((8, 128), jnp.int32),
            pltpu.VMEM((REST, 128), F32),
            dma((4,)),
            dma((24,)),
            dma((32,)),
            dma((32,)),
            dma((32,)),
            dma((9,)),
            dma((2,)),
        ],
        compiler_params=pltpu.CompilerParams(collective_id=0, has_side_effects=True, vmem_limit_bytes=10 * 2**20),
        name="gather",
    )(in_hbm(factor_rows[0]), in_hbm(parent_tiles), front_sizes, in_hbm(tile_counts))
    part = pl.pallas_call(
        tiles_kernel,
        out_shape=jax.ShapeDtypeStruct((TRASH + 1, TR, TR), F32),
        in_specs=[smem, smem, smem, vmem, vmem, vmem],
        out_specs=vmem,
        scratch_shapes=[pltpu.SMEM((2 * REST + UNROLL,), jnp.int32)],
        compiler_params=pltpu.CompilerParams(vmem_limit_bytes=4 * 2**20),
        name="tiles",
    )(codes, rest, totals, split, reused, staged)
    summed = pl.pallas_call(
        scatter_kernel,
        out_shape=jax.ShapeDtypeStruct((8, TR, TR), F32),
        in_specs=[vmem],
        out_specs=vmem,
        scratch_shapes=[
            pltpu.VMEM((2, 2, 8, TR, TR), F32),
            pltpu.VMEM((2, 2, 16, TR, TR), F32),
            pltpu.VMEM((2, 2, 8, TR, TR), F32),
            pltpu.VMEM((2, 16, TR, TR), F32),
            pltpu.VMEM((2, 2, 2, TR, TR), F32),
            pltpu.VMEM((2, 2, 4, TR, TR), F32),
            pltpu.VMEM((2, 2, 2, TR, TR), F32),
            dma((24,)),
            dma((24,)),
        ],
        compiler_params=pltpu.CompilerParams(collective_id=1, has_side_effects=True, vmem_limit_bytes=14 * 2**20),
        name="scatter",
    )(part)
    return parent_entries - summed


def solution(mesh):
    in_specs = (P("front", "blk", None), P("front"), P(), P(), P(("front", "blk"), None, None))
    out_specs = P(("front", "blk"), None, None)
    return jax.shard_map(
        per_device, mesh=mesh, in_specs=in_specs, out_specs=out_specs, check_vma=False
    )
```

```python
import functools

import jax
import jax.numpy as jnp
from jax import lax
from jax.experimental import pallas as pl
from jax.experimental.pallas import tpu as pltpu
from jax.sharding import PartitionSpec as P

TR = 128
KH = 512
CB = 4
EB = 32
UNROLL = 8
BATCH = 16
FIXED = (48, 24, 28, 16)
REUSED = 40
FREED = (20, 21, 22, 23, 28, 29, 30, 31)
BEGIN = (0, 8, 32)
REST = 256
TRASH = 128

MESH = pl.DeviceIdType.MESH
F32 = jnp.float32
BF16 = jnp.bfloat16


def position():
    front, blk = lax.axis_index("front"), lax.axis_index("blk")
    return dict(
        front=front,
        blk=blk,
        y=front // 4,
        xl=(front // 2) % 2,
        core=front % 2,
        xh=blk // 4,
        z=blk % 4,
    )


def device(p, **moves):
    q = {**p, **moves}
    return {"front": q["y"] * 4 + q["xl"] * 2 + q["core"], "blk": q["xh"] * 4 + q["z"]}


def slot(xs, dz, c):
    return (xs * 4 + dz) * CB + c


def gather_kernel(
    x, parents, sizes, counts, split, other, staged, codes, rest, totals,
    mine, fs, fs_other, targets, count_s, code_s, rows_by_place,
    x_send, z_send, recv, core_send, core_recv, local, fs_sem,
):
    p = position()
    z, xh = p["z"], p["xh"]
    up, down = device(p, z=(z + 1) % 4), device(p, z=(z + 3) % 4)
    across = device(p, xh=1 - xh)
    twin = device(p, core=1 - p["core"])

    fronts = [(p["front"] // 2) * 2 + (p["core"] if g == 0 else 1 - p["core"]) for g in range(2)]
    small = [
        pltpu.make_async_copy(counts, count_s, local.at[5]),
        pltpu.make_async_copy(parents.at[fronts[0]], targets.at[0], local.at[6]),
        pltpu.make_async_copy(parents.at[fronts[1]], targets.at[1], local.at[7]),
    ]
    for copy in small:
        copy.start()
    barrier = pltpu.get_barrier_semaphore()
    for other_dev in (up, down, across, twin):
        pl.semaphore_signal(barrier, inc=1, device_id=other_dev, device_id_type=MESH)
    pl.semaphore_wait(barrier, 4)

    sent = []

    def send(src, dst, ssem, rsem, to):
        copy = pltpu.make_async_remote_copy(
            src_ref=src, dst_ref=dst, send_sem=ssem, recv_sem=rsem, device_id=to, device_id_type=MESH
        )
        copy.start()
        sent.append(copy)

    n_z = [0]

    def send_z(src, xs, dz, c, to):
        s = slot(xs, dz, c)
        send(src, mine.at[s], z_send.at[n_z[0]], recv.at[s], to)
        n_z[0] += 1

    def arrived(s):
        pltpu.make_async_remote_copy(
            src_ref=mine.at[s], dst_ref=mine.at[s], send_sem=z_send.at[0], recv_sem=recv.at[s],
            device_id=up, device_id_type=MESH,
        ).wait_recv()

    def to_twin(s):
        send(mine.at[s], other.at[s], core_send.at[s], core_recv.at[s], twin)

    def from_twin(s):
        pltpu.make_async_remote_copy(
            src_ref=mine.at[s], dst_ref=other.at[s], send_sem=core_send.at[s], recv_sem=core_recv.at[s],
            device_id=twin, device_id_type=MESH,
        ).wait_recv()

    own_cols = pl.ds(pl.multiple_of(xh * KH, KH), KH)
    across_cols = pl.ds(pl.multiple_of((1 - xh) * KH, KH), KH)

    def rows(c):
        return pl.ds(c * TR, TR)

    fs[...] = jnp.full((8, KH), sizes[0], jnp.int32)
    loads = []
    for c in (0, 2, 1, 3):
        s = slot(1, 0, c)
        send(x.at[rows(c), across_cols], mine.at[s], x_send.at[c], recv.at[s], across)
    for c, d in ((0, 2), (1, 3), (2, 0), (3, 1)):
        send_z(x.at[rows(c), own_cols], 0, 3, c, up)
        send_z(x.at[rows(d), own_cols], 0, 1, d, down)
        load = pltpu.make_async_copy(x.at[rows(c), own_cols], mine.at[slot(0, 0, c)], local.at[c])
        load.start()
        loads.append(load)

    for copy in small:
        copy.wait()
    send(fs, fs_other, fs_sem.at[0], fs_sem.at[1], twin)
    fs_copy = sent[-1]

    col = lax.broadcasted_iota(jnp.int32, (EB, EB), 1)
    row = lax.broadcasted_iota(jnp.int32, (EB, EB), 0)
    lower = (row >= col).astype(F32)
    before = (row < col).astype(F32)

    def place_of(block):
        return ((((block >> 4) ^ xh) << 4) + ((((block >> 2) - z) & 3) << 2)) + (block & 3)

    def level_of(s):
        return jnp.where(s < 20, 0, jnp.where((s >= 24) & (s < 28), 3, 1) + (s & 1))

    a_slot, b_slot = place_of(row), place_of(col)
    level = jnp.maximum(level_of(a_slot), level_of(b_slot))

    def places(hit):
        rank = jnp.dot(lower, hit.astype(F32), preferred_element_type=F32)
        many = jnp.broadcast_to(rank[EB - 1 : EB, :], (8, EB))
        start = jnp.dot(many, before, preferred_element_type=F32)
        at = (rank + start[0:1, :]).astype(jnp.int32) - 1
        return jnp.where(hit, at, -1), jnp.sum(many[0:1, :], axis=1, keepdims=True).astype(jnp.int32)

    ones = jnp.full((8, EB), 1.0, F32)

    def listed(at, code, size):
        def eight(i, _):
            first = pl.multiple_of(i * 8, 8)
            for k in range(8):
                rows_by_place[pl.ds(first + k, 1), 0:EB] = jnp.sum(
                    jnp.where(at == first + k, code, 0.0), axis=0, keepdims=True
                )
            return 0

        whole = (size + 7) // 8 * 8
        lax.fori_loop(0, whole // 8, eight, 0)
        found = lax.dot_general(
            ones, rows_by_place[0:whole, 0:EB], (((1,), (1,)), ((), ())),
            precision=lax.Precision.HIGHEST, preferred_element_type=F32,
        )
        return found[0:1, 0:size].astype(jnp.int32)

    def plan(g):
        target = targets[g]
        live = count_s[fronts[g]]
        dest = target >> 3
        dest_front, dest_blk = dest >> 3, dest & 7
        hit = ((dest_blk & 3) == z) & ((dest_front & 1) == p["core"])
        hit = hit & (row < live) & (col < live)
        rx = ((dest_blk >> 2) * 2 + ((dest_front >> 1) & 1) - (p["xh"] * 2 + p["xl"])) & 3
        ry = ((dest_front >> 2) - p["y"]) & 3
        place = target & 7
        first = place < 4
        at = jnp.where(first, ry * 4 + rx, 16 + rx * 4 + ry) * 4 + (place & 3)
        code = ((b_slot << 13) + (a_slot << 8) + at).astype(F32)
        over = level == 4
        for n in range(4):
            where, many = places(hit & (level == n))
            codes[g * 4 + n : g * 4 + n + 1, 0 : FIXED[n]] = listed(where, code, FIXED[n])
            totals[g * 8 + n : g * 8 + n + 1, :] = jnp.broadcast_to(many, (1, 128))
            over = over | (where >= FIXED[n])
        where, many = places(hit & over)
        rest[g : g + 1, :] = listed(where, code, REST)
        totals[g * 8 + 4 : g * 8 + 5, :] = jnp.broadcast_to(many, (1, 128))

    def product(g, n, t):
        c = code_s[g * 4 + n, t]
        d = lax.dot_general(
            split[g, (c >> 8) & 31], split[g, (c >> 13) & 31], (((1,), (1,)), ((), ())),
            preferred_element_type=F32,
        )
        return d[:TR, :TR] + (d[:TR, TR:] + d[TR:, :TR])

    def products(g, n, begin, end):
        for t in range(begin, end):
            lanes = pl.ds((t % 4) * TR, TR)
            if n == 3:
                other[FREED[g * 4 + t // 4], :, lanes] = product(g, n, t)
            elif n == 0 and t < REUSED:
                other[g * 10 + t // 4, :, lanes] = product(g, n, t)
            else:
                staged[g, BEGIN[n] + t - (REUSED if n == 0 else 0)] = product(g, n, t)

    def convert(g, s):
        src = mine if g == 0 else other
        size = (fs if g == 0 else fs_other)[0:1, :]
        block = lax.broadcasted_iota(jnp.int32, (1, KH), 1) // TR + xh * (KH // TR)
        keep = block < size

        def step(i, _):
            at = pl.multiple_of(i * 16, 16)
            v = jnp.where(keep, src[s, pl.ds(at, 16), :], 0.0)
            hi = v.astype(BF16)
            split[g, s, pl.ds(at, 16), :] = hi
            split[g, s, pl.ds(TR + at, 16), :] = (v - hi.astype(F32)).astype(BF16)
            return 0

        lax.fori_loop(0, TR // 16, step, 0)

    twin_queue = []

    def take(s):
        to_twin(s)
        convert(0, s)
        twin_queue.append(s)
        if len(twin_queue) > 4:
            drain()

    def drain():
        t = twin_queue.pop(0)
        from_twin(t)
        convert(1, t)

    plan(0)
    fs_copy.wait_recv()
    for c, load in zip((0, 1, 2, 3), loads):
        load.wait()
        take(slot(0, 0, c))
    for i in range(4):
        c, d = (0, 1, 2, 3)[i], (2, 3, 0, 1)[i]
        arrived(slot(0, 3, c))
        if c < 2:
            send_z(mine.at[slot(0, 3, c)], 0, 2, c, up)
        take(slot(0, 3, c))
        arrived(slot(0, 1, d))
        if d >= 2:
            send_z(mine.at[slot(0, 1, d)], 0, 2, d, down)
        take(slot(0, 1, d))
        e = (0, 2, 1, 3)[i]
        s = slot(1, 0, e)
        arrived(s)
        send_z(mine.at[s], 1, 3, e, up)
        send_z(mine.at[s], 1, 1, e, down)
        take(s)
        if i == 0:
            plan(1)
        if i == 2:
            code_copy = pltpu.make_async_copy(codes, code_s, local.at[8])
            code_copy.start()
    for e in (0, 2, 1, 3):
        arrived(slot(0, 2, e))
        take(slot(0, 2, e))
    code_copy.wait()
    while twin_queue:
        drain()
    work = [(0, 0), (1, 0), (0, 1), (1, 1), (0, 2), (1, 2)]

    def batch():
        g, first = work.pop(0)
        products(g, 0, first * BATCH, (first + 1) * BATCH)

    for e in (0, 2, 1, 3):
        s = slot(1, 3, e)
        arrived(s)
        if e < 2:
            send_z(mine.at[s], 1, 2, e, up)
        take(s)
        s = slot(1, 1, e)
        arrived(s)
        if e >= 2:
            send_z(mine.at[s], 1, 2, e, down)
        take(s)
        if e in (0, 2):
            batch()
            batch()
        if e == 2:
            while twin_queue:
                drain()
            batch()
            batch()
        if e in (1, 3):
            products(0 if e == 1 else 1, 1, 0, FIXED[1])
    while twin_queue:
        drain()
    products(0, 2, 0, FIXED[2])
    for e in (0, 2):
        arrived(slot(1, 2, e))
        take(slot(1, 2, e))
    products(1, 2, 0, FIXED[2])
    while twin_queue:
        drain()
    products(0, 3, 0, FIXED[3])
    products(1, 3, 0, FIXED[3])
    for e in (1, 3):
        arrived(slot(1, 2, e))
        take(slot(1, 2, e))
    while twin_queue:
        drain()
    for copy in sent:
        copy.wait_send()


def tiles_kernel(codes, rest, totals, held, reused, staged, acc, flat):
    def clear(i, _):
        acc[i] = jnp.zeros((TR, TR), F32)
        return 0

    lax.fori_loop(0, TRASH + 1, clear, 0)
    def add(g, n, t, value):
        at = jnp.where(t < totals[g * 8 + n, 0], codes[g * 4 + n, t] & 255, TRASH)
        acc[at] += value

    for g in range(2):
        def four(i, _):
            for u in range(4):
                add(g, 0, i * 4 + u, reused[g * 10 + i, :, pl.ds(u * TR, TR)])
            return 0

        lax.fori_loop(0, REUSED // 4, four, 0)
        for t in range(REUSED, FIXED[0]):
            add(g, 0, t, staged[g, t - REUSED])

        for n in (1, 2):
            def some(i, _):
                for u in range(4):
                    add(g, n, i * 4 + u, staged[g, BEGIN[n] + i * 4 + u])
                return 0

            lax.fori_loop(0, FIXED[n] // 4, some, 0)
        for t in range(FIXED[3]):
            add(g, 3, t, reused[FREED[g * 4 + t // 4], :, pl.ds((t % 4) * TR, TR)])
    count = 0
    for g in range(2):
        def entry(k, _):
            flat[count + k] = rest[g, k] + (g << 18)
            return 0

        lax.fori_loop(0, totals[g * 8 + 4, 0], entry, 0)
        count = count + totals[g * 8 + 4, 0]
    for u in range(UNROLL - 1):
        flat[count + u] = TRASH

    def several(i, _):
        for u in range(UNROLL):
            c = flat[i * UNROLL + u]
            g, b, a, at = c >> 18, (c >> 13) & 31, (c >> 8) & 31, c & 255
            d = lax.dot_general(
                held[g, a], held[g, b], (((1,), (1,)), ((), ())), preferred_element_type=F32
            )
            acc[at] += d[:TR, :TR] + (d[:TR, TR:] + d[TR:, :TR])
        return 0

    lax.fori_loop(0, (count + UNROLL - 1) // UNROLL, several, 0)


def scatter_kernel(
    part, out, opp, near, fwd, mid, mid_opp, mid_near, mid_fwd,
    send_sem, recv_sem,
):
    p = position()
    x = p["xh"] * 2 + p["xl"]

    def along_x(d):
        n = (x + d) % 4
        return device(p, xh=n // 2, xl=n % 2)

    def along_y(d):
        return device(p, y=(p["y"] + d) % 4)

    barrier = pltpu.get_barrier_semaphore()
    for to in (along_x(1), along_x(3), along_y(1), along_y(3)):
        pl.semaphore_signal(barrier, inc=1, device_id=to, device_id_type=MESH)
    pl.semaphore_wait(barrier, 4)

    sent = []
    count = [0]

    def send(src, dst, to):
        k = count[0]
        count[0] += 1
        copy = pltpu.make_async_remote_copy(
            src_ref=src, dst_ref=dst, send_sem=send_sem.at[k], recv_sem=recv_sem.at[k],
            device_id=to, device_id_type=MESH,
        )
        copy.start()
        sent.append(copy)
        return copy

    def begin(src, n, h, to, opp, near):
        half = n // 2
        o_up = send(src(2, 0, half), opp.at[h, 0], to(1))
        o_down = send(src(2, half, half), opp.at[h, 1], to(3))
        n_up = send(src(1, half, half), near.at[h, 0, pl.ds(half, half)], to(1))
        n_down = send(src(3, 0, half), near.at[h, 1, pl.ds(0, half)], to(3))
        return o_up, o_down, n_up, n_down

    def relay(copies, val, h, to):
        late = []
        copies[0].wait_recv()
        for lo in (4, 0):
            fwd[h, 0, pl.ds(lo, 4)] = val(1, lo, 4) + opp[h, 0, pl.ds(lo, 4)]
            late.append(send(fwd.at[h, 0, pl.ds(lo, 4)], near.at[h, 0, pl.ds(lo, 4)], to(1)))
        copies[1].wait_recv()
        for lo in (0, 4):
            fwd[h, 1, pl.ds(lo, 4)] = val(3, 8 + lo, 4) + opp[h, 1, pl.ds(lo, 4)]
            late.append(send(fwd.at[h, 1, pl.ds(lo, 4)], near.at[h, 1, pl.ds(8 + lo, 4)], to(3)))
        return [copies[2], copies[3]] + late

    ways = ((along_y, along_x), (along_x, along_y))

    def value(h):
        return lambda r, lo, size: part[pl.ds(h * 64 + r * 16 + lo, size)]

    firsts = []
    for h in range(2):
        firsts.append(
            begin(lambda r, lo, size: part.at[pl.ds(h * 64 + r * 16 + lo, size)], 16, h, ways[h][0], opp, near)
        )
    for h in range(2):
        firsts[h] = relay(firsts[h], value(h), h, ways[h][0])

    def settle(h, r):
        at = pl.ds(r * 4, 4)
        mid[h, at] = part[pl.ds(h * 64 + r * 4, 4)] + (near[h, 0, at] + near[h, 1, at])

    seconds = []
    for h in range(2):
        to = ways[h][1]
        n_up, n_down, up_1, up_0, down_2, down_3 = firsts[h]
        n_up.wait_recv()
        n_down.wait_recv()
        down_2.wait_recv()
        settle(h, 2)
        two = [
            send(mid.at[h, pl.ds(8, 2)], mid_opp.at[h, 0], to(1)),
            send(mid.at[h, pl.ds(10, 2)], mid_opp.at[h, 1], to(3)),
        ]
        up_1.wait_recv()
        settle(h, 1)
        two.append(send(mid.at[h, pl.ds(6, 2)], mid_near.at[h, 0, pl.ds(2, 2)], to(1)))
        seconds.append(two)
    for h in range(2):
        to = ways[h][1]
        n_up, n_down, up_1, up_0, down_2, down_3 = firsts[h]
        down_3.wait_recv()
        settle(h, 3)
        seconds[h].append(send(mid.at[h, pl.ds(12, 2)], mid_near.at[h, 1, pl.ds(0, 2)], to(3)))
    ends = []
    for h in range(2):
        to = ways[h][1]
        o_up, o_down, n_up, n_down = seconds[h]
        o_up.wait_recv()
        mid_fwd[h, 0] = mid[h, pl.ds(4, 2)] + mid_opp[h, 0]
        f_up = send(mid_fwd.at[h, 0], mid_near.at[h, 0, pl.ds(0, 2)], to(1))
        o_down.wait_recv()
        mid_fwd[h, 1] = mid[h, pl.ds(14, 2)] + mid_opp[h, 1]
        f_down = send(mid_fwd.at[h, 1], mid_near.at[h, 1, pl.ds(2, 2)], to(3))
        ends.append((n_up, n_down, f_up, f_down))
    for h in range(2):
        firsts[h][3].wait_recv()
        settle(h, 0)
    for h in range(2):
        for copy in ends[h]:
            copy.wait_recv()
        out[pl.ds(h * 4, 4)] = mid[h, pl.ds(0, 4)] + (mid_near[h, 0] + mid_near[h, 1])
    for copy in sent:
        copy.wait_send()


def per_device(factor_rows, front_sizes, tile_counts, parent_tiles, parent_entries):
    vmem = pl.BlockSpec(memory_space=pltpu.VMEM)
    smem = pl.BlockSpec(memory_space=pltpu.SMEM)
    dma = pltpu.SemaphoreType.DMA
    hbm = pl.BlockSpec(memory_space=pltpu.HBM)

    def in_hbm(a):
        return pltpu.with_memory_space_constraint(a, pltpu.HBM)

    split, reused, staged, codes, rest, totals = pl.pallas_call(
        gather_kernel,
        out_shape=(
            jax.ShapeDtypeStruct((2, EB, 2 * TR, KH), BF16),
            jax.ShapeDtypeStruct((EB, TR, KH), F32),
            jax.ShapeDtypeStruct((2, BEGIN[2] + FIXED[2], TR, TR), F32),
            jax.ShapeDtypeStruct((8, 128), jnp.int32),
            jax.ShapeDtypeStruct((8, REST), jnp.int32),
            jax.ShapeDtypeStruct((16, 128), jnp.int32),
        ),
        in_specs=[hbm, hbm, smem, hbm],
        out_specs=(vmem,) * 6,
        scratch_shapes=[
            pltpu.VMEM((EB, TR, KH), F32),
            pltpu.VMEM((8, KH), jnp.int32),
            pltpu.VMEM((8, KH), jnp.int32),
            pltpu.VMEM((2, EB, EB), jnp.int32),
            pltpu.SMEM((16,), jnp.int32),
            pltpu.SMEM((8, 128), jnp.int32),
            pltpu.VMEM((REST, 128), F32),
            dma((4,)),
            dma((24,)),
            dma((32,)),
            dma((32,)),
            dma((32,)),
            dma((9,)),
            dma((2,)),
        ],
        compiler_params=pltpu.CompilerParams(collective_id=0, has_side_effects=True, vmem_limit_bytes=10 * 2**20),
        name="gather",
    )(in_hbm(factor_rows[0]), in_hbm(parent_tiles), front_sizes, in_hbm(tile_counts))
    part = pl.pallas_call(
        tiles_kernel,
        out_shape=jax.ShapeDtypeStruct((TRASH + 1, TR, TR), F32),
        in_specs=[smem, smem, smem, vmem, vmem, vmem],
        out_specs=vmem,
        scratch_shapes=[pltpu.SMEM((2 * REST + UNROLL,), jnp.int32)],
        compiler_params=pltpu.CompilerParams(vmem_limit_bytes=4 * 2**20),
        name="tiles",
    )(codes, rest, totals, split, reused, staged)
    summed = pl.pallas_call(
        scatter_kernel,
        out_shape=jax.ShapeDtypeStruct((8, TR, TR), F32),
        in_specs=[vmem],
        out_specs=vmem,
        scratch_shapes=[
            pltpu.VMEM((2, 2, 8, TR, TR), F32),
            pltpu.VMEM((2, 2, 16, TR, TR), F32),
            pltpu.VMEM((2, 2, 8, TR, TR), F32),
            pltpu.VMEM((2, 16, TR, TR), F32),
            pltpu.VMEM((2, 2, 2, TR, TR), F32),
            pltpu.VMEM((2, 2, 4, TR, TR), F32),
            pltpu.VMEM((2, 2, 2, TR, TR), F32),
            dma((28,)),
            dma((28,)),
        ],
        compiler_params=pltpu.CompilerParams(collective_id=1, has_side_effects=True, vmem_limit_bytes=14 * 2**20),
        name="scatter",
    )(part)
    return parent_entries - summed


def solution(mesh):
    in_specs = (P("front", "blk", None), P("front"), P(), P(), P(("front", "blk"), None, None))
    out_specs = P(("front", "blk"), None, None)
    return jax.shard_map(
        per_device, mesh=mesh, in_specs=in_specs, out_specs=out_specs, check_vma=False
    )
```

```python
import functools

import jax
import jax.numpy as jnp
from jax import lax
from jax.experimental import pallas as pl
from jax.experimental.pallas import tpu as pltpu
from jax.sharding import PartitionSpec as P

TR = 128
KH = 512
CB = 4
EB = 32
UNROLL = 8
FIXED = (16, 32, 24, 28, 20)
LEVELS = len(FIXED)
STAGED = 64
REST = 256
TRASH = 128

MESH = pl.DeviceIdType.MESH
F32 = jnp.float32
BF16 = jnp.bfloat16


def homes(g):
    return (
        (0, 0, 16, True, g * 4),
        (1, 0, 24, True, 8 + g * 6),
        (1, 24, 8, False, 0),
        (2, 0, 24, False, 8),
        (3, 0, 28, False, 32),
        (4, 0, 16, True, 20 + g * 8),
        (4, 16, 4, False, 60),
    )


def position():
    front, blk = lax.axis_index("front"), lax.axis_index("blk")
    return dict(
        front=front,
        blk=blk,
        y=front // 4,
        xl=(front // 2) % 2,
        core=front % 2,
        xh=blk // 4,
        z=blk % 4,
    )


def device(p, **moves):
    q = {**p, **moves}
    return {"front": q["y"] * 4 + q["xl"] * 2 + q["core"], "blk": q["xh"] * 4 + q["z"]}


def slot(xs, dz, c):
    return (xs * 4 + dz) * CB + c


def gather_kernel(
    x, parents, sizes, counts, split, other, staged, codes, rest, totals,
    mine, fs, fs_other, targets, count_s, code_s, rows_by_place,
    x_send, z_send, recv, core_send, core_recv, local, fs_sem,
):
    p = position()
    z, xh = p["z"], p["xh"]
    up, down = device(p, z=(z + 1) % 4), device(p, z=(z + 3) % 4)
    across = device(p, xh=1 - xh)
    twin = device(p, core=1 - p["core"])

    fronts = [(p["front"] // 2) * 2 + (p["core"] if g == 0 else 1 - p["core"]) for g in range(2)]
    small = [
        pltpu.make_async_copy(counts, count_s, local.at[5]),
        pltpu.make_async_copy(parents.at[fronts[0]], targets.at[0], local.at[6]),
        pltpu.make_async_copy(parents.at[fronts[1]], targets.at[1], local.at[7]),
    ]
    for copy in small:
        copy.start()
    barrier = pltpu.get_barrier_semaphore()
    for other_dev in (up, down, across, twin):
        pl.semaphore_signal(barrier, inc=1, device_id=other_dev, device_id_type=MESH)
    pl.semaphore_wait(barrier, 4)

    sent = []

    def send(src, dst, ssem, rsem, to):
        copy = pltpu.make_async_remote_copy(
            src_ref=src, dst_ref=dst, send_sem=ssem, recv_sem=rsem, device_id=to, device_id_type=MESH
        )
        copy.start()
        sent.append(copy)

    n_z = [0]

    def send_z(src, xs, dz, c, to):
        s = slot(xs, dz, c)
        send(src, mine.at[s], z_send.at[n_z[0]], recv.at[s], to)
        n_z[0] += 1

    def arrived(s):
        pltpu.make_async_remote_copy(
            src_ref=mine.at[s], dst_ref=mine.at[s], send_sem=z_send.at[0], recv_sem=recv.at[s],
            device_id=up, device_id_type=MESH,
        ).wait_recv()

    def to_twin(s):
        send(mine.at[s], other.at[s], core_send.at[s], core_recv.at[s], twin)

    def from_twin(s):
        pltpu.make_async_remote_copy(
            src_ref=mine.at[s], dst_ref=other.at[s], send_sem=core_send.at[s], recv_sem=core_recv.at[s],
            device_id=twin, device_id_type=MESH,
        ).wait_recv()

    own_cols = pl.ds(pl.multiple_of(xh * KH, KH), KH)
    across_cols = pl.ds(pl.multiple_of((1 - xh) * KH, KH), KH)

    def rows(c):
        return pl.ds(c * TR, TR)

    fs[...] = jnp.full((8, KH), sizes[0], jnp.int32)
    loads = []
    for c in (0, 2, 1, 3):
        s = slot(1, 0, c)
        send(x.at[rows(c), across_cols], mine.at[s], x_send.at[c], recv.at[s], across)
    for c, d in ((0, 2), (1, 3), (2, 0), (3, 1)):
        send_z(x.at[rows(c), own_cols], 0, 3, c, up)
        send_z(x.at[rows(d), own_cols], 0, 1, d, down)
        load = pltpu.make_async_copy(x.at[rows(c), own_cols], mine.at[slot(0, 0, c)], local.at[c])
        load.start()
        loads.append(load)

    for copy in small:
        copy.wait()
    send(fs, fs_other, fs_sem.at[0], fs_sem.at[1], twin)
    fs_copy = sent[-1]

    col = lax.broadcasted_iota(jnp.int32, (EB, EB), 1)
    row = lax.broadcasted_iota(jnp.int32, (EB, EB), 0)
    lower = (row >= col).astype(F32)
    before = (row < col).astype(F32)

    def place_of(block):
        return ((((block >> 4) ^ xh) << 4) + ((((block >> 2) - z) & 3) << 2)) + (block & 3)

    def level_of(s):
        early = jnp.where((s < 8) | ((s >= 12) & (s < 16)), 0, 1)
        return jnp.where(s < 20, early, jnp.where((s >= 24) & (s < 28), 4, 2) + (s & 1))

    a_slot, b_slot = place_of(row), place_of(col)
    level = jnp.maximum(level_of(a_slot), level_of(b_slot))

    def places(hit):
        rank = jnp.dot(lower, hit.astype(F32), preferred_element_type=F32)
        many = jnp.broadcast_to(rank[EB - 1 : EB, :], (8, EB))
        start = jnp.dot(many, before, preferred_element_type=F32)
        at = (rank + start[0:1, :]).astype(jnp.int32) - 1
        return jnp.where(hit, at, -1), jnp.sum(many[0:1, :], axis=1, keepdims=True).astype(jnp.int32)

    ones = jnp.full((8, EB), 1.0, F32)

    def listed(at, code, size):
        def eight(i, _):
            first = pl.multiple_of(i * 8, 8)
            for k in range(8):
                rows_by_place[pl.ds(first + k, 1), 0:EB] = jnp.sum(
                    jnp.where(at == first + k, code, 0.0), axis=0, keepdims=True
                )
            return 0

        whole = (size + 7) // 8 * 8
        lax.fori_loop(0, whole // 8, eight, 0)
        found = lax.dot_general(
            ones, rows_by_place[0:whole, 0:EB], (((1,), (1,)), ((), ())),
            precision=lax.Precision.HIGHEST, preferred_element_type=F32,
        )
        return found[0:1, 0:size].astype(jnp.int32)

    def plan(g):
        target = targets[g]
        live = count_s[fronts[g]]
        dest = target >> 3
        dest_front, dest_blk = dest >> 3, dest & 7
        hit = ((dest_blk & 3) == z) & ((dest_front & 1) == p["core"])
        hit = hit & (row < live) & (col < live)
        rx = ((dest_blk >> 2) * 2 + ((dest_front >> 1) & 1) - (p["xh"] * 2 + p["xl"])) & 3
        ry = ((dest_front >> 2) - p["y"]) & 3
        place = target & 7
        first = place < 4
        at = jnp.where(first, ry * 4 + rx, 16 + rx * 4 + ry) * 4 + (place & 3)
        code = ((b_slot << 13) + (a_slot << 8) + at).astype(F32)
        late = hit & (level == LEVELS)
        over = hit & (level < 0)
        for n in range(LEVELS):
            where, many = places((hit & (level == n)) | over)
            codes[g * 8 + n : g * 8 + n + 1, 0 : FIXED[n]] = listed(where, code, FIXED[n])
            totals[g * 8 + n : g * 8 + n + 1, :] = jnp.broadcast_to(many, (1, 128))
            over = where >= FIXED[n]
        where, many = places(late | over)
        rest[g : g + 1, :] = listed(where, code, REST)
        totals[g * 8 + LEVELS : g * 8 + LEVELS + 1, :] = jnp.broadcast_to(many, (1, 128))

    def product(g, n, t):
        c = code_s[g * 8 + n, t]
        d = lax.dot_general(
            split[g, (c >> 8) & 31], split[g, (c >> 13) & 31], (((1,), (1,)), ((), ())),
            preferred_element_type=F32,
        )
        return d[:TR, :TR] + (d[:TR, TR:] + d[TR:, :TR])

    def products(g, n):
        for level_, first, many, again, base in homes(g):
            if level_ == n:
                for t in range(many):
                    d = product(g, n, first + t)
                    if again:
                        other[base + t // 4, :, pl.ds((t % 4) * TR, TR)] = d
                    else:
                        staged[g, base + t] = d

    def convert(g, s):
        src = mine if g == 0 else other
        size = (fs if g == 0 else fs_other)[0:1, :]
        block = lax.broadcasted_iota(jnp.int32, (1, KH), 1) // TR + xh * (KH // TR)
        keep = block < size

        def step(i, _):
            at = pl.multiple_of(i * 16, 16)
            v = jnp.where(keep, src[s, pl.ds(at, 16), :], 0.0)
            hi = v.astype(BF16)
            split[g, s, pl.ds(at, 16), :] = hi
            split[g, s, pl.ds(TR + at, 16), :] = (v - hi.astype(F32)).astype(BF16)
            return 0

        lax.fori_loop(0, TR // 16, step, 0)

    twin_queue = []

    def take(s):
        to_twin(s)
        convert(0, s)
        twin_queue.append(s)
        if len(twin_queue) > 4:
            drain()

    def drain():
        t = twin_queue.pop(0)
        from_twin(t)
        convert(1, t)

    plan(0)
    def drain_all():
        while twin_queue:
            drain()

    fs_copy.wait_recv()
    for c, load in zip((0, 1, 2, 3), loads):
        load.wait()
        take(slot(0, 0, c))
    for i in range(4):
        c, d = (0, 1, 2, 3)[i], (2, 3, 0, 1)[i]
        arrived(slot(0, 3, c))
        if c < 2:
            send_z(mine.at[slot(0, 3, c)], 0, 2, c, up)
        take(slot(0, 3, c))
        arrived(slot(0, 1, d))
        if d >= 2:
            send_z(mine.at[slot(0, 1, d)], 0, 2, d, down)
        take(slot(0, 1, d))
        if i == 3:
            code_copy.wait()
            drain_all()
            products(0, 0)
            products(1, 0)
        e = (0, 2, 1, 3)[i]
        s = slot(1, 0, e)
        arrived(s)
        send_z(mine.at[s], 1, 3, e, up)
        send_z(mine.at[s], 1, 1, e, down)
        take(s)
        if i == 0:
            plan(1)
        if i == 1:
            code_copy = pltpu.make_async_copy(codes, code_s, local.at[8])
            code_copy.start()
    for e in (0, 2, 1, 3):
        arrived(slot(0, 2, e))
        take(slot(0, 2, e))
    drain_all()
    for e in (0, 2, 1, 3):
        s = slot(1, 3, e)
        arrived(s)
        if e < 2:
            send_z(mine.at[s], 1, 2, e, up)
        take(s)
        s = slot(1, 1, e)
        arrived(s)
        if e >= 2:
            send_z(mine.at[s], 1, 2, e, down)
        take(s)
        if e == 0:
            products(0, 1)
        if e == 2:
            products(1, 1)
            drain_all()
        if e == 1:
            products(0, 2)
        if e == 3:
            products(1, 2)
    drain_all()
    products(0, 3)
    for e in (0, 2):
        arrived(slot(1, 2, e))
        take(slot(1, 2, e))
    products(1, 3)
    drain_all()
    products(0, 4)
    products(1, 4)
    for e in (1, 3):
        arrived(slot(1, 2, e))
        take(slot(1, 2, e))
    drain_all()
    for copy in sent:
        copy.wait_send()


def tiles_kernel(codes, rest, totals, held, reused, staged, acc, flat):
    def clear(i, _):
        acc[i] = jnp.zeros((TR, TR), F32)
        return 0

    lax.fori_loop(0, TRASH + 1, clear, 0)
    for g in range(2):
        for n, first, many, again, base in homes(g):
            wide = 8 if many % 8 == 0 else 4
            total = totals[g * 8 + n, 0]

            def some(i, _):
                for u in range(wide):
                    t = first + i * wide + u
                    at = jnp.where(t < total, codes[g * 8 + n, t] & 255, TRASH)
                    if again:
                        acc[at] += reused[base + i * (wide // 4) + u // 4, :, pl.ds((u % 4) * TR, TR)]
                    else:
                        acc[at] += staged[g, base + i * wide + u]
                return 0

            lax.fori_loop(0, many // wide, some, 0)
    count = 0
    for g in range(2):
        def entry(k, _):
            flat[count + k] = rest[g, k] + (g << 18)
            return 0

        lax.fori_loop(0, totals[g * 8 + LEVELS, 0], entry, 0)
        count = count + totals[g * 8 + LEVELS, 0]
    for u in range(UNROLL - 1):
        flat[count + u] = TRASH

    def several(i, _):
        for u in range(UNROLL):
            c = flat[i * UNROLL + u]
            g, b, a, at = c >> 18, (c >> 13) & 31, (c >> 8) & 31, c & 255
            d = lax.dot_general(
                held[g, a], held[g, b], (((1,), (1,)), ((), ())), preferred_element_type=F32
            )
            acc[at] += d[:TR, :TR] + (d[:TR, TR:] + d[TR:, :TR])
        return 0

    lax.fori_loop(0, (count + UNROLL - 1) // UNROLL, several, 0)


def scatter_kernel(
    part, out, opp, near, fwd, mid, mid_opp, mid_near, mid_fwd,
    send_sem, recv_sem,
):
    p = position()
    x = p["xh"] * 2 + p["xl"]

    def along_x(d):
        n = (x + d) % 4
        return device(p, xh=n // 2, xl=n % 2)

    def along_y(d):
        return device(p, y=(p["y"] + d) % 4)

    barrier = pltpu.get_barrier_semaphore()
    for to in (along_x(1), along_x(3), along_y(1), along_y(3)):
        pl.semaphore_signal(barrier, inc=1, device_id=to, device_id_type=MESH)
    pl.semaphore_wait(barrier, 4)

    sent = []
    count = [0]

    def send(src, dst, to):
        k = count[0]
        count[0] += 1
        copy = pltpu.make_async_remote_copy(
            src_ref=src, dst_ref=dst, send_sem=send_sem.at[k], recv_sem=recv_sem.at[k],
            device_id=to, device_id_type=MESH,
        )
        copy.start()
        sent.append(copy)
        return copy

    def begin(src, n, h, to, opp, near):
        half = n // 2
        o_up = send(src(2, 0, half), opp.at[h, 0], to(1))
        o_down = send(src(2, half, half), opp.at[h, 1], to(3))
        n_up = send(src(1, half, half), near.at[h, 0, pl.ds(half, half)], to(1))
        n_down = send(src(3, 0, half), near.at[h, 1, pl.ds(0, half)], to(3))
        return o_up, o_down, n_up, n_down

    def relay(copies, val, h, to):
        late = []
        copies[0].wait_recv()
        for lo in (4, 0):
            fwd[h, 0, pl.ds(lo, 4)] = val(1, lo, 4) + opp[h, 0, pl.ds(lo, 4)]
            late.append(send(fwd.at[h, 0, pl.ds(lo, 4)], near.at[h, 0, pl.ds(lo, 4)], to(1)))
        copies[1].wait_recv()
        for lo in (0, 4):
            fwd[h, 1, pl.ds(lo, 4)] = val(3, 8 + lo, 4) + opp[h, 1, pl.ds(lo, 4)]
            late.append(send(fwd.at[h, 1, pl.ds(lo, 4)], near.at[h, 1, pl.ds(8 + lo, 4)], to(3)))
        return [copies[2], copies[3]] + late

    ways = ((along_y, along_x), (along_x, along_y))

    def value(h):
        return lambda r, lo, size: part[pl.ds(h * 64 + r * 16 + lo, size)]

    firsts = []
    for h in range(2):
        firsts.append(
            begin(lambda r, lo, size: part.at[pl.ds(h * 64 + r * 16 + lo, size)], 16, h, ways[h][0], opp, near)
        )
    for h in range(2):
        firsts[h] = relay(firsts[h], value(h), h, ways[h][0])

    def settle(h, r):
        at = pl.ds(r * 4, 4)
        mid[h, at] = part[pl.ds(h * 64 + r * 4, 4)] + (near[h, 0, at] + near[h, 1, at])

    seconds = []
    for h in range(2):
        to = ways[h][1]
        n_up, n_down, up_1, up_0, down_2, down_3 = firsts[h]
        n_up.wait_recv()
        n_down.wait_recv()
        down_2.wait_recv()
        settle(h, 2)
        two = [
            send(mid.at[h, pl.ds(8, 2)], mid_opp.at[h, 0], to(1)),
            send(mid.at[h, pl.ds(10, 2)], mid_opp.at[h, 1], to(3)),
        ]
        up_1.wait_recv()
        settle(h, 1)
        two.append(send(mid.at[h, pl.ds(6, 2)], mid_near.at[h, 0, pl.ds(2, 2)], to(1)))
        seconds.append(two)
    for h in range(2):
        to = ways[h][1]
        n_up, n_down, up_1, up_0, down_2, down_3 = firsts[h]
        down_3.wait_recv()
        settle(h, 3)
        seconds[h].append(send(mid.at[h, pl.ds(12, 2)], mid_near.at[h, 1, pl.ds(0, 2)], to(3)))
    ends = []
    for h in range(2):
        to = ways[h][1]
        o_up, o_down, n_up, n_down = seconds[h]
        o_up.wait_recv()
        mid_fwd[h, 0] = mid[h, pl.ds(4, 2)] + mid_opp[h, 0]
        f_up = send(mid_fwd.at[h, 0], mid_near.at[h, 0, pl.ds(0, 2)], to(1))
        o_down.wait_recv()
        mid_fwd[h, 1] = mid[h, pl.ds(14, 2)] + mid_opp[h, 1]
        f_down = send(mid_fwd.at[h, 1], mid_near.at[h, 1, pl.ds(2, 2)], to(3))
        ends.append((n_up, n_down, f_up, f_down))
    for h in range(2):
        firsts[h][3].wait_recv()
        settle(h, 0)
    for h in range(2):
        for copy in ends[h]:
            copy.wait_recv()
        out[pl.ds(h * 4, 4)] = mid[h, pl.ds(0, 4)] + (mid_near[h, 0] + mid_near[h, 1])
    for copy in sent:
        copy.wait_send()


def per_device(factor_rows, front_sizes, tile_counts, parent_tiles, parent_entries):
    vmem = pl.BlockSpec(memory_space=pltpu.VMEM)
    smem = pl.BlockSpec(memory_space=pltpu.SMEM)
    dma = pltpu.SemaphoreType.DMA
    hbm = pl.BlockSpec(memory_space=pltpu.HBM)

    def in_hbm(a):
        return pltpu.with_memory_space_constraint(a, pltpu.HBM)

    split, reused, staged, codes, rest, totals = pl.pallas_call(
        gather_kernel,
        out_shape=(
            jax.ShapeDtypeStruct((2, EB, 2 * TR, KH), BF16),
            jax.ShapeDtypeStruct((EB, TR, KH), F32),
            jax.ShapeDtypeStruct((2, STAGED, TR, TR), F32),
            jax.ShapeDtypeStruct((16, 128), jnp.int32),
            jax.ShapeDtypeStruct((8, REST), jnp.int32),
            jax.ShapeDtypeStruct((16, 128), jnp.int32),
        ),
        in_specs=[hbm, hbm, smem, hbm],
        out_specs=(vmem,) * 6,
        scratch_shapes=[
            pltpu.VMEM((EB, TR, KH), F32),
            pltpu.VMEM((8, KH), jnp.int32),
            pltpu.VMEM((8, KH), jnp.int32),
            pltpu.VMEM((2, EB, EB), jnp.int32),
            pltpu.SMEM((16,), jnp.int32),
            pltpu.SMEM((16, 128), jnp.int32),
            pltpu.VMEM((REST, 128), F32),
            dma((4,)),
            dma((24,)),
            dma((32,)),
            dma((32,)),
            dma((32,)),
            dma((9,)),
            dma((2,)),
        ],
        compiler_params=pltpu.CompilerParams(collective_id=0, has_side_effects=True, vmem_limit_bytes=10 * 2**20),
        name="gather",
    )(in_hbm(factor_rows[0]), in_hbm(parent_tiles), front_sizes, in_hbm(tile_counts))
    part = pl.pallas_call(
        tiles_kernel,
        out_shape=jax.ShapeDtypeStruct((TRASH + 1, TR, TR), F32),
        in_specs=[smem, smem, smem, vmem, vmem, vmem],
        out_specs=vmem,
        scratch_shapes=[pltpu.SMEM((2 * REST + UNROLL,), jnp.int32)],
        compiler_params=pltpu.CompilerParams(vmem_limit_bytes=4 * 2**20),
        name="tiles",
    )(codes, rest, totals, split, reused, staged)
    summed = pl.pallas_call(
        scatter_kernel,
        out_shape=jax.ShapeDtypeStruct((8, TR, TR), F32),
        in_specs=[vmem],
        out_specs=vmem,
        scratch_shapes=[
            pltpu.VMEM((2, 2, 8, TR, TR), F32),
            pltpu.VMEM((2, 2, 16, TR, TR), F32),
            pltpu.VMEM((2, 2, 8, TR, TR), F32),
            pltpu.VMEM((2, 16, TR, TR), F32),
            pltpu.VMEM((2, 2, 2, TR, TR), F32),
            pltpu.VMEM((2, 2, 4, TR, TR), F32),
            pltpu.VMEM((2, 2, 2, TR, TR), F32),
            dma((28,)),
            dma((28,)),
        ],
        compiler_params=pltpu.CompilerParams(collective_id=1, has_side_effects=True, vmem_limit_bytes=14 * 2**20),
        name="scatter",
    )(part)
    return parent_entries - summed


def solution(mesh):
    in_specs = (P("front", "blk", None), P("front"), P(), P(), P(("front", "blk"), None, None))
    out_specs = P(("front", "blk"), None, None)
    return jax.shard_map(
        per_device, mesh=mesh, in_specs=in_specs, out_specs=out_specs, check_vma=False
    )
```

```python
import functools

import jax
import jax.numpy as jnp
from jax import lax
from jax.experimental import pallas as pl
from jax.experimental.pallas import tpu as pltpu
from jax.sharding import PartitionSpec as P

TR = 128
KH = 512
CB = 4
EB = 32
UNROLL = 8
MERGED = 4
FIXED = (16, 32, 24, 28, 20)
LEVELS = len(FIXED)
STAGED = 64
REST = 256
TRASH = 128

MESH = pl.DeviceIdType.MESH
F32 = jnp.float32
BF16 = jnp.bfloat16


def homes(g):
    return (
        (0, 0, 16, True, g * 4),
        (1, 0, 24, True, 8 + g * 6),
        (1, 24, 8, False, 0),
        (2, 0, 24, False, 8),
        (3, 0, 28, False, 32),
        (4, 0, 16, True, 20 + g * 8),
        (4, 16, 4, False, 60),
    )


def position():
    front, blk = lax.axis_index("front"), lax.axis_index("blk")
    return dict(
        front=front,
        blk=blk,
        y=front // 4,
        xl=(front // 2) % 2,
        core=front % 2,
        xh=blk // 4,
        z=blk % 4,
    )


def device(p, **moves):
    q = {**p, **moves}
    return {"front": q["y"] * 4 + q["xl"] * 2 + q["core"], "blk": q["xh"] * 4 + q["z"]}


def slot(xs, dz, c):
    return (xs * 4 + dz) * CB + c


def gather_kernel(
    x, parents, sizes, counts, split, other, staged, codes, rest, totals,
    mine, fs, fs_other, targets, count_s, code_s, rows_by_place,
    x_send, z_send, recv, core_send, core_recv, local, fs_sem,
):
    p = position()
    z, xh = p["z"], p["xh"]
    up, down = device(p, z=(z + 1) % 4), device(p, z=(z + 3) % 4)
    across = device(p, xh=1 - xh)
    twin = device(p, core=1 - p["core"])

    fronts = [(p["front"] // 2) * 2 + (p["core"] if g == 0 else 1 - p["core"]) for g in range(2)]
    small = [
        pltpu.make_async_copy(counts, count_s, local.at[5]),
        pltpu.make_async_copy(parents.at[fronts[0]], targets.at[0], local.at[6]),
        pltpu.make_async_copy(parents.at[fronts[1]], targets.at[1], local.at[7]),
    ]
    for copy in small:
        copy.start()
    barrier = pltpu.get_barrier_semaphore()
    for other_dev in (up, down, across, twin):
        pl.semaphore_signal(barrier, inc=1, device_id=other_dev, device_id_type=MESH)
    pl.semaphore_wait(barrier, 4)

    sent = []

    def send(src, dst, ssem, rsem, to):
        copy = pltpu.make_async_remote_copy(
            src_ref=src, dst_ref=dst, send_sem=ssem, recv_sem=rsem, device_id=to, device_id_type=MESH
        )
        copy.start()
        sent.append(copy)

    n_z = [0]

    def send_z(src, xs, dz, c, to):
        s = slot(xs, dz, c)
        send(src, mine.at[s], z_send.at[n_z[0]], recv.at[s], to)
        n_z[0] += 1

    def arrived(s):
        pltpu.make_async_remote_copy(
            src_ref=mine.at[s], dst_ref=mine.at[s], send_sem=z_send.at[0], recv_sem=recv.at[s],
            device_id=up, device_id_type=MESH,
        ).wait_recv()

    def to_twin(s):
        send(mine.at[s], other.at[s], core_send.at[s], core_recv.at[s], twin)

    def from_twin(s):
        pltpu.make_async_remote_copy(
            src_ref=mine.at[s], dst_ref=other.at[s], send_sem=core_send.at[s], recv_sem=core_recv.at[s],
            device_id=twin, device_id_type=MESH,
        ).wait_recv()

    own_cols = pl.ds(pl.multiple_of(xh * KH, KH), KH)
    across_cols = pl.ds(pl.multiple_of((1 - xh) * KH, KH), KH)

    def rows(c):
        return pl.ds(c * TR, TR)

    fs[...] = jnp.full((8, KH), sizes[0], jnp.int32)
    loads = []
    for c in (0, 2, 1, 3):
        s = slot(1, 0, c)
        send(x.at[rows(c), across_cols], mine.at[s], x_send.at[c], recv.at[s], across)
    for c, d in ((0, 2), (1, 3), (2, 0), (3, 1)):
        send_z(x.at[rows(c), own_cols], 0, 3, c, up)
        send_z(x.at[rows(d), own_cols], 0, 1, d, down)
        load = pltpu.make_async_copy(x.at[rows(c), own_cols], mine.at[slot(0, 0, c)], local.at[c])
        load.start()
        loads.append(load)

    for copy in small:
        copy.wait()
    send(fs, fs_other, fs_sem.at[0], fs_sem.at[1], twin)
    fs_copy = sent[-1]

    col = lax.broadcasted_iota(jnp.int32, (EB, EB), 1)
    row = lax.broadcasted_iota(jnp.int32, (EB, EB), 0)
    lower = (row >= col).astype(F32)
    before = (row < col).astype(F32)

    def place_of(block):
        return ((((block >> 4) ^ xh) << 4) + ((((block >> 2) - z) & 3) << 2)) + (block & 3)

    def level_of(s):
        early = jnp.where((s < 8) | ((s >= 12) & (s < 16)), 0, 1)
        return jnp.where(s < 20, early, jnp.where((s >= 24) & (s < 28), 4, 2) + (s & 1))

    a_slot, b_slot = place_of(row), place_of(col)
    level = jnp.maximum(level_of(a_slot), level_of(b_slot))

    def places(hit):
        rank = jnp.dot(lower, hit.astype(F32), preferred_element_type=F32)
        many = jnp.broadcast_to(rank[EB - 1 : EB, :], (8, EB))
        start = jnp.dot(many, before, preferred_element_type=F32)
        at = (rank + start[0:1, :]).astype(jnp.int32) - 1
        return jnp.where(hit, at, -1), jnp.sum(many[0:1, :], axis=1, keepdims=True).astype(jnp.int32)

    ones = jnp.full((8, EB), 1.0, F32)

    def listed(at, code, size):
        def eight(i, _):
            first = pl.multiple_of(i * 8, 8)
            for k in range(8):
                rows_by_place[pl.ds(first + k, 1), 0:EB] = jnp.sum(
                    jnp.where(at == first + k, code, 0.0), axis=0, keepdims=True
                )
            return 0

        whole = (size + 7) // 8 * 8
        lax.fori_loop(0, whole // 8, eight, 0)
        found = lax.dot_general(
            ones, rows_by_place[0:whole, 0:EB], (((1,), (1,)), ((), ())),
            precision=lax.Precision.HIGHEST, preferred_element_type=F32,
        )
        return found[0:1, 0:size].astype(jnp.int32)

    def plan(g):
        target = targets[g]
        live = count_s[fronts[g]]
        dest = target >> 3
        dest_front, dest_blk = dest >> 3, dest & 7
        hit = ((dest_blk & 3) == z) & ((dest_front & 1) == p["core"])
        hit = hit & (row < live) & (col < live)
        rx = ((dest_blk >> 2) * 2 + ((dest_front >> 1) & 1) - (p["xh"] * 2 + p["xl"])) & 3
        ry = ((dest_front >> 2) - p["y"]) & 3
        place = target & 7
        first = place < 4
        at = jnp.where(first, ry * 4 + rx, 16 + rx * 4 + ry) * 4 + (place & 3)
        code = ((b_slot << 13) + (a_slot << 8) + at).astype(F32)
        late = hit & (level == LEVELS)
        over = hit & (level < 0)
        for n in range(LEVELS):
            where, many = places((hit & (level == n)) | over)
            codes[g * 8 + n : g * 8 + n + 1, 0 : FIXED[n]] = listed(where, code, FIXED[n])
            totals[g * 8 + n : g * 8 + n + 1, :] = jnp.broadcast_to(many, (1, 128))
            over = where >= FIXED[n]
        where, many = places(late | over)
        rest[g : g + 1, :] = listed(where, code, REST)
        totals[g * 8 + LEVELS : g * 8 + LEVELS + 1, :] = jnp.broadcast_to(many, (1, 128))

    def product(g, n, t):
        c = code_s[g * 8 + n, t]
        d = lax.dot_general(
            split[g, (c >> 8) & 31], split[g, (c >> 13) & 31], (((1,), (1,)), ((), ())),
            preferred_element_type=F32,
        )
        return d[:TR, :TR] + (d[:TR, TR:] + d[TR:, :TR])

    def products(g, n):
        for level_, first, many, again, base in homes(g):
            if level_ == n:
                for t in range(many):
                    d = product(g, n, first + t)
                    if again:
                        other[base + t // 4, :, pl.ds((t % 4) * TR, TR)] = d
                    else:
                        staged[g, base + t] = d

    def convert(g, s):
        src = mine if g == 0 else other
        size = (fs if g == 0 else fs_other)[0:1, :]
        block = lax.broadcasted_iota(jnp.int32, (1, KH), 1) // TR + xh * (KH // TR)
        keep = block < size

        def step(i, _):
            at = pl.multiple_of(i * 16, 16)
            v = jnp.where(keep, src[s, pl.ds(at, 16), :], 0.0)
            hi = v.astype(BF16)
            split[g, s, pl.ds(at, 16), :] = hi
            split[g, s, pl.ds(TR + at, 16), :] = (v - hi.astype(F32)).astype(BF16)
            return 0

        lax.fori_loop(0, TR // 16, step, 0)

    twin_queue = []

    def take(s):
        to_twin(s)
        convert(0, s)
        twin_queue.append(s)
        if len(twin_queue) > 4:
            drain()

    def drain():
        t = twin_queue.pop(0)
        from_twin(t)
        convert(1, t)

    plan(0)
    def drain_all():
        while twin_queue:
            drain()

    fs_copy.wait_recv()
    for c, load in zip((0, 1, 2, 3), loads):
        load.wait()
        take(slot(0, 0, c))
    for i in range(4):
        c, d = (0, 1, 2, 3)[i], (2, 3, 0, 1)[i]
        arrived(slot(0, 3, c))
        if c < 2:
            send_z(mine.at[slot(0, 3, c)], 0, 2, c, up)
        take(slot(0, 3, c))
        arrived(slot(0, 1, d))
        if d >= 2:
            send_z(mine.at[slot(0, 1, d)], 0, 2, d, down)
        take(slot(0, 1, d))
        if i == 3:
            code_copy.wait()
            drain_all()
            products(0, 0)
            products(1, 0)
        e = (0, 2, 1, 3)[i]
        s = slot(1, 0, e)
        arrived(s)
        send_z(mine.at[s], 1, 3, e, up)
        send_z(mine.at[s], 1, 1, e, down)
        take(s)
        if i == 0:
            plan(1)
        if i == 1:
            code_copy = pltpu.make_async_copy(codes, code_s, local.at[8])
            code_copy.start()
    for e in (0, 2, 1, 3):
        arrived(slot(0, 2, e))
        take(slot(0, 2, e))
    drain_all()
    for e in (0, 2, 1, 3):
        s = slot(1, 3, e)
        arrived(s)
        if e < 2:
            send_z(mine.at[s], 1, 2, e, up)
        take(s)
        s = slot(1, 1, e)
        arrived(s)
        if e >= 2:
            send_z(mine.at[s], 1, 2, e, down)
        take(s)
        if e == 0:
            products(0, 1)
        if e == 2:
            products(1, 1)
            drain_all()
        if e == 1:
            products(0, 2)
        if e == 3:
            products(1, 2)
    drain_all()
    products(0, 3)
    for e in (0, 2):
        arrived(slot(1, 2, e))
        take(slot(1, 2, e))
    products(1, 3)
    drain_all()
    products(0, 4)
    products(1, 4)
    for e in (1, 3):
        arrived(slot(1, 2, e))
        take(slot(1, 2, e))
    drain_all()
    for copy in sent:
        copy.wait_send()


def tiles_kernel(codes, rest, totals, held, reused, staged, acc, flat):
    def clear(i, _):
        acc[i] = jnp.zeros((TR, TR), F32)
        return 0

    lax.fori_loop(0, TRASH + 1, clear, 0)
    count = 0
    for g in range(2):
        def entry(k, _):
            flat[count + k] = rest[g, k] + (g << 18)
            return 0

        lax.fori_loop(0, totals[g * 8 + LEVELS, 0], entry, 0)
        count = count + totals[g * 8 + LEVELS, 0]

    def blank(k, _):
        flat[k] = TRASH
        return 0

    lax.fori_loop(count, jnp.maximum(count + UNROLL, MERGED * UNROLL), blank, 0)

    def add(g, n, t, value):
        at = jnp.where(t < totals[g * 8 + n, 0], codes[g * 8 + n, t] & 255, TRASH)
        acc[at] += value

    def fixed(g, n, first, again, base, per, i, u):
        t = first + i * per + u
        if again:
            add(g, n, t, reused[base + i * (per // 4) + u // 4, :, pl.ds((u % 4) * TR, TR)])
        else:
            add(g, n, t, staged[g, base + i * per + u])

    def rest_tile(t):
        c = flat[t]
        g, b, a, at = c >> 18, (c >> 13) & 31, (c >> 8) & 31, c & 255
        d = lax.dot_general(
            held[g, a], held[g, b], (((1,), (1,)), ((), ())), preferred_element_type=F32
        )
        return at, d

    def put(at, d):
        acc[at] += d[:TR, :TR] + (d[:TR, TR:] + d[TR:, :TR])

    runs, odd = [], []
    for g in range(2):
        for n, first, many, again, base in homes(g):
            grain = 4 * MERGED if again else MERGED
            even = many // grain * grain
            runs += [(g, n, first, again, base, even // MERGED, u) for u in range(even // MERGED)]
            odd += [(g, n, first + t, again, base + (t // 4 if again else t), t % 4 if again else 0) for t in range(even, many)]

    def merged(i, _):
        share = -(-len(runs) // UNROLL)
        for k in range(UNROLL):
            at, d = rest_tile(i * UNROLL + k)
            for g, n, first, again, base, per, u in runs[k * share : (k + 1) * share]:
                fixed(g, n, first, again, base, per, i, u)
            put(at, d)
        return 0

    lax.fori_loop(0, MERGED, merged, 0)
    for g, n, t, again, place, lane in odd:
        add(g, n, t, reused[place, :, pl.ds(lane * TR, TR)] if again else staged[g, place])

    def several(i, _):
        for k in range(UNROLL):
            put(*rest_tile(i * UNROLL + k))
        return 0

    lax.fori_loop(MERGED, (count + UNROLL - 1) // UNROLL, several, 0)


def scatter_kernel(
    part, out, opp, near, fwd, mid, mid_opp, mid_near, mid_fwd,
    send_sem, recv_sem,
):
    p = position()
    x = p["xh"] * 2 + p["xl"]

    def along_x(d):
        n = (x + d) % 4
        return device(p, xh=n // 2, xl=n % 2)

    def along_y(d):
        return device(p, y=(p["y"] + d) % 4)

    barrier = pltpu.get_barrier_semaphore()
    for to in (along_x(1), along_x(3), along_y(1), along_y(3)):
        pl.semaphore_signal(barrier, inc=1, device_id=to, device_id_type=MESH)
    pl.semaphore_wait(barrier, 4)

    sent = []
    count = [0]

    def send(src, dst, to):
        k = count[0]
        count[0] += 1
        copy = pltpu.make_async_remote_copy(
            src_ref=src, dst_ref=dst, send_sem=send_sem.at[k], recv_sem=recv_sem.at[k],
            device_id=to, device_id_type=MESH,
        )
        copy.start()
        sent.append(copy)
        return copy

    def begin(src, n, h, to, opp, near):
        half = n // 2
        o_up = send(src(2, 0, half), opp.at[h, 0], to(1))
        o_down = send(src(2, half, half), opp.at[h, 1], to(3))
        n_up = send(src(1, half, half), near.at[h, 0, pl.ds(half, half)], to(1))
        n_down = send(src(3, 0, half), near.at[h, 1, pl.ds(0, half)], to(3))
        return o_up, o_down, n_up, n_down

    def relay(copies, val, h, to):
        late = []
        copies[0].wait_recv()
        for lo in (4, 0):
            fwd[h, 0, pl.ds(lo, 4)] = val(1, lo, 4) + opp[h, 0, pl.ds(lo, 4)]
            late.append(send(fwd.at[h, 0, pl.ds(lo, 4)], near.at[h, 0, pl.ds(lo, 4)], to(1)))
        copies[1].wait_recv()
        for lo in (0, 4):
            fwd[h, 1, pl.ds(lo, 4)] = val(3, 8 + lo, 4) + opp[h, 1, pl.ds(lo, 4)]
            late.append(send(fwd.at[h, 1, pl.ds(lo, 4)], near.at[h, 1, pl.ds(8 + lo, 4)], to(3)))
        return [copies[2], copies[3]] + late

    ways = ((along_y, along_x), (along_x, along_y))

    def value(h):
        return lambda r, lo, size: part[pl.ds(h * 64 + r * 16 + lo, size)]

    firsts = []
    for h in range(2):
        firsts.append(
            begin(lambda r, lo, size: part.at[pl.ds(h * 64 + r * 16 + lo, size)], 16, h, ways[h][0], opp, near)
        )
    for h in range(2):
        firsts[h] = relay(firsts[h], value(h), h, ways[h][0])

    def settle(h, r):
        at = pl.ds(r * 4, 4)
        mid[h, at] = part[pl.ds(h * 64 + r * 4, 4)] + (near[h, 0, at] + near[h, 1, at])

    seconds = []
    for h in range(2):
        to = ways[h][1]
        n_up, n_down, up_1, up_0, down_2, down_3 = firsts[h]
        n_up.wait_recv()
        n_down.wait_recv()
        down_2.wait_recv()
        settle(h, 2)
        two = [
            send(mid.at[h, pl.ds(8, 2)], mid_opp.at[h, 0], to(1)),
            send(mid.at[h, pl.ds(10, 2)], mid_opp.at[h, 1], to(3)),
        ]
        up_1.wait_recv()
        settle(h, 1)
        two.append(send(mid.at[h, pl.ds(6, 2)], mid_near.at[h, 0, pl.ds(2, 2)], to(1)))
        seconds.append(two)
    for h in range(2):
        to = ways[h][1]
        n_up, n_down, up_1, up_0, down_2, down_3 = firsts[h]
        down_3.wait_recv()
        settle(h, 3)
        seconds[h].append(send(mid.at[h, pl.ds(12, 2)], mid_near.at[h, 1, pl.ds(0, 2)], to(3)))
    ends = []
    for h in range(2):
        to = ways[h][1]
        o_up, o_down, n_up, n_down = seconds[h]
        o_up.wait_recv()
        mid_fwd[h, 0] = mid[h, pl.ds(4, 2)] + mid_opp[h, 0]
        f_up = send(mid_fwd.at[h, 0], mid_near.at[h, 0, pl.ds(0, 2)], to(1))
        o_down.wait_recv()
        mid_fwd[h, 1] = mid[h, pl.ds(14, 2)] + mid_opp[h, 1]
        f_down = send(mid_fwd.at[h, 1], mid_near.at[h, 1, pl.ds(2, 2)], to(3))
        ends.append((n_up, n_down, f_up, f_down))
    for h in range(2):
        firsts[h][3].wait_recv()
        settle(h, 0)
    for h in range(2):
        for copy in ends[h]:
            copy.wait_recv()
        out[pl.ds(h * 4, 4)] = mid[h, pl.ds(0, 4)] + (mid_near[h, 0] + mid_near[h, 1])
    for copy in sent:
        copy.wait_send()


def per_device(factor_rows, front_sizes, tile_counts, parent_tiles, parent_entries):
    vmem = pl.BlockSpec(memory_space=pltpu.VMEM)
    smem = pl.BlockSpec(memory_space=pltpu.SMEM)
    dma = pltpu.SemaphoreType.DMA
    hbm = pl.BlockSpec(memory_space=pltpu.HBM)

    def in_hbm(a):
        return pltpu.with_memory_space_constraint(a, pltpu.HBM)

    split, reused, staged, codes, rest, totals = pl.pallas_call(
        gather_kernel,
        out_shape=(
            jax.ShapeDtypeStruct((2, EB, 2 * TR, KH), BF16),
            jax.ShapeDtypeStruct((EB, TR, KH), F32),
            jax.ShapeDtypeStruct((2, STAGED, TR, TR), F32),
            jax.ShapeDtypeStruct((16, 128), jnp.int32),
            jax.ShapeDtypeStruct((8, REST), jnp.int32),
            jax.ShapeDtypeStruct((16, 128), jnp.int32),
        ),
        in_specs=[hbm, hbm, smem, hbm],
        out_specs=(vmem,) * 6,
        scratch_shapes=[
            pltpu.VMEM((EB, TR, KH), F32),
            pltpu.VMEM((8, KH), jnp.int32),
            pltpu.VMEM((8, KH), jnp.int32),
            pltpu.VMEM((2, EB, EB), jnp.int32),
            pltpu.SMEM((16,), jnp.int32),
            pltpu.SMEM((16, 128), jnp.int32),
            pltpu.VMEM((REST, 128), F32),
            dma((4,)),
            dma((24,)),
            dma((32,)),
            dma((32,)),
            dma((32,)),
            dma((9,)),
            dma((2,)),
        ],
        compiler_params=pltpu.CompilerParams(collective_id=0, has_side_effects=True, vmem_limit_bytes=10 * 2**20),
        name="gather",
    )(in_hbm(factor_rows[0]), in_hbm(parent_tiles), front_sizes, in_hbm(tile_counts))
    part = pl.pallas_call(
        tiles_kernel,
        out_shape=jax.ShapeDtypeStruct((TRASH + 1, TR, TR), F32),
        in_specs=[smem, smem, smem, vmem, vmem, vmem],
        out_specs=vmem,
        scratch_shapes=[pltpu.SMEM((2 * REST + MERGED * UNROLL,), jnp.int32)],
        compiler_params=pltpu.CompilerParams(vmem_limit_bytes=4 * 2**20),
        name="tiles",
    )(codes, rest, totals, split, reused, staged)
    summed = pl.pallas_call(
        scatter_kernel,
        out_shape=jax.ShapeDtypeStruct((8, TR, TR), F32),
        in_specs=[vmem],
        out_specs=vmem,
        scratch_shapes=[
            pltpu.VMEM((2, 2, 8, TR, TR), F32),
            pltpu.VMEM((2, 2, 16, TR, TR), F32),
            pltpu.VMEM((2, 2, 8, TR, TR), F32),
            pltpu.VMEM((2, 16, TR, TR), F32),
            pltpu.VMEM((2, 2, 2, TR, TR), F32),
            pltpu.VMEM((2, 2, 4, TR, TR), F32),
            pltpu.VMEM((2, 2, 2, TR, TR), F32),
            dma((28,)),
            dma((28,)),
        ],
        compiler_params=pltpu.CompilerParams(collective_id=1, has_side_effects=True, vmem_limit_bytes=14 * 2**20),
        name="scatter",
    )(part)
    return parent_entries - summed


def solution(mesh):
    in_specs = (P("front", "blk", None), P("front"), P(), P(), P(("front", "blk"), None, None))
    out_specs = P(("front", "blk"), None, None)
    return jax.shard_map(
        per_device, mesh=mesh, in_specs=in_specs, out_specs=out_specs, check_vma=False
    )
```

```python
import functools

import jax
import jax.numpy as jnp
from jax import lax
from jax.experimental import pallas as pl
from jax.experimental.pallas import tpu as pltpu
from jax.sharding import PartitionSpec as P

TR = 128
KH = 512
CB = 4
EB = 32
UNROLL = 8
MERGED = 4
FIXED = (16, 32, 24, 28, 20)
LEVELS = len(FIXED)
STAGED = 64
REST = 256
TRASH = 128

MESH = pl.DeviceIdType.MESH
F32 = jnp.float32
BF16 = jnp.bfloat16


def homes(g):
    return (
        (0, 0, 16, True, g * 4),
        (1, 0, 24, True, 8 + g * 6),
        (1, 24, 8, False, 0),
        (2, 0, 24, False, 8),
        (3, 0, 28, False, 32),
        (4, 0, 16, True, 20 + g * 8),
        (4, 16, 4, False, 60),
    )


def position():
    front, blk = lax.axis_index("front"), lax.axis_index("blk")
    return dict(
        front=front,
        blk=blk,
        y=front // 4,
        xl=(front // 2) % 2,
        core=front % 2,
        xh=blk // 4,
        z=blk % 4,
    )


def device(p, **moves):
    q = {**p, **moves}
    return {"front": q["y"] * 4 + q["xl"] * 2 + q["core"], "blk": q["xh"] * 4 + q["z"]}


def slot(xs, dz, c):
    return (xs * 4 + dz) * CB + c


def gather_kernel(
    x, parents, sizes, counts, split, other, staged, codes, rest, totals,
    mine, fs, fs_other, targets, count_s, code_s, rows_by_place,
    x_send, z_send, recv, core_send, core_recv, local, fs_sem,
):
    p = position()
    z, xh = p["z"], p["xh"]
    up, down = device(p, z=(z + 1) % 4), device(p, z=(z + 3) % 4)
    across = device(p, xh=1 - xh)
    twin = device(p, core=1 - p["core"])

    fronts = [(p["front"] // 2) * 2 + (p["core"] if g == 0 else 1 - p["core"]) for g in range(2)]
    small = [
        pltpu.make_async_copy(counts, count_s, local.at[5]),
        pltpu.make_async_copy(parents.at[fronts[0]], targets.at[0], local.at[6]),
        pltpu.make_async_copy(parents.at[fronts[1]], targets.at[1], local.at[7]),
    ]
    for copy in small:
        copy.start()
    barrier = pltpu.get_barrier_semaphore()
    for other_dev in (up, down, across, twin):
        pl.semaphore_signal(barrier, inc=1, device_id=other_dev, device_id_type=MESH)
    pl.semaphore_wait(barrier, 4)

    sent = []

    def send(src, dst, ssem, rsem, to):
        copy = pltpu.make_async_remote_copy(
            src_ref=src, dst_ref=dst, send_sem=ssem, recv_sem=rsem, device_id=to, device_id_type=MESH
        )
        copy.start()
        sent.append(copy)

    n_z = [0]

    def send_z(src, xs, dz, c, to):
        s = slot(xs, dz, c)
        send(src, mine.at[s], z_send.at[n_z[0]], recv.at[s], to)
        n_z[0] += 1

    def arrived(s):
        pltpu.make_async_remote_copy(
            src_ref=mine.at[s], dst_ref=mine.at[s], send_sem=z_send.at[0], recv_sem=recv.at[s],
            device_id=up, device_id_type=MESH,
        ).wait_recv()

    def to_twin(s):
        send(mine.at[s], other.at[s], core_send.at[s], core_recv.at[s], twin)

    def from_twin(s):
        pltpu.make_async_remote_copy(
            src_ref=mine.at[s], dst_ref=other.at[s], send_sem=core_send.at[s], recv_sem=core_recv.at[s],
            device_id=twin, device_id_type=MESH,
        ).wait_recv()

    own_cols = pl.ds(pl.multiple_of(xh * KH, KH), KH)
    across_cols = pl.ds(pl.multiple_of((1 - xh) * KH, KH), KH)

    def rows(c):
        return pl.ds(c * TR, TR)

    fs[...] = jnp.full((8, KH), sizes[0], jnp.int32)
    loads = []
    for c, d in ((0, 2), (1, 3), (2, 0), (3, 1)):
        send_z(x.at[rows(c), own_cols], 0, 3, c, up)
        send_z(x.at[rows(d), own_cols], 0, 1, d, down)
        load = pltpu.make_async_copy(x.at[rows(c), own_cols], mine.at[slot(0, 0, c)], local.at[c])
        load.start()
        loads.append(load)

    for c in (0, 2, 1, 3):
        s = slot(1, 0, c)
        send(x.at[rows(c), across_cols], mine.at[s], x_send.at[c], recv.at[s], across)
    for copy in small:
        copy.wait()
    send(fs, fs_other, fs_sem.at[0], fs_sem.at[1], twin)
    fs_copy = sent[-1]

    col = lax.broadcasted_iota(jnp.int32, (EB, EB), 1)
    row = lax.broadcasted_iota(jnp.int32, (EB, EB), 0)
    lower = (row >= col).astype(F32)
    before = (row < col).astype(F32)

    def place_of(block):
        return ((((block >> 4) ^ xh) << 4) + ((((block >> 2) - z) & 3) << 2)) + (block & 3)

    def level_of(s):
        early = jnp.where((s < 8) | ((s >= 12) & (s < 16)), 0, 1)
        return jnp.where(s < 20, early, jnp.where((s >= 24) & (s < 28), 4, 2) + (s & 1))

    a_slot, b_slot = place_of(row), place_of(col)
    level = jnp.maximum(level_of(a_slot), level_of(b_slot))

    def places(hit):
        rank = jnp.dot(lower, hit.astype(F32), preferred_element_type=F32)
        many = jnp.broadcast_to(rank[EB - 1 : EB, :], (8, EB))
        start = jnp.dot(many, before, preferred_element_type=F32)
        at = (rank + start[0:1, :]).astype(jnp.int32) - 1
        return jnp.where(hit, at, -1), jnp.sum(many[0:1, :], axis=1, keepdims=True).astype(jnp.int32)

    ones = jnp.full((8, EB), 1.0, F32)

    def listed(at, code, size):
        def eight(i, _):
            first = pl.multiple_of(i * 8, 8)
            for k in range(8):
                rows_by_place[pl.ds(first + k, 1), 0:EB] = jnp.sum(
                    jnp.where(at == first + k, code, 0.0), axis=0, keepdims=True
                )
            return 0

        whole = (size + 7) // 8 * 8
        lax.fori_loop(0, whole // 8, eight, 0)
        found = lax.dot_general(
            ones, rows_by_place[0:whole, 0:EB], (((1,), (1,)), ((), ())),
            precision=lax.Precision.HIGHEST, preferred_element_type=F32,
        )
        return found[0:1, 0:size].astype(jnp.int32)

    def plan(g):
        target = targets[g]
        live = count_s[fronts[g]]
        dest = target >> 3
        dest_front, dest_blk = dest >> 3, dest & 7
        hit = ((dest_blk & 3) == z) & ((dest_front & 1) == p["core"])
        hit = hit & (row < live) & (col < live)
        rx = ((dest_blk >> 2) * 2 + ((dest_front >> 1) & 1) - (p["xh"] * 2 + p["xl"])) & 3
        ry = ((dest_front >> 2) - p["y"]) & 3
        place = target & 7
        first = place < 4
        at = jnp.where(first, ry * 4 + rx, 16 + rx * 4 + ry) * 4 + (place & 3)
        code = ((b_slot << 13) + (a_slot << 8) + at).astype(F32)
        late = hit & (level == LEVELS)
        over = hit & (level < 0)
        for n in range(LEVELS):
            where, many = places((hit & (level == n)) | over)
            codes[g * 8 + n : g * 8 + n + 1, 0 : FIXED[n]] = listed(where, code, FIXED[n])
            totals[g * 8 + n : g * 8 + n + 1, :] = jnp.broadcast_to(many, (1, 128))
            over = where >= FIXED[n]
        where, many = places(late | over)
        rest[g : g + 1, :] = listed(where, code, REST)
        totals[g * 8 + LEVELS : g * 8 + LEVELS + 1, :] = jnp.broadcast_to(many, (1, 128))

    def product(g, n, t):
        c = code_s[g * 8 + n, t]
        d = lax.dot_general(
            split[g, (c >> 8) & 31], split[g, (c >> 13) & 31], (((1,), (1,)), ((), ())),
            preferred_element_type=F32,
        )
        return d[:TR, :TR] + (d[:TR, TR:] + d[TR:, :TR])

    def products(g, n):
        for level_, first, many, again, base in homes(g):
            if level_ == n:
                for t in range(many):
                    d = product(g, n, first + t)
                    if again:
                        other[base + t // 4, :, pl.ds((t % 4) * TR, TR)] = d
                    else:
                        staged[g, base + t] = d

    def convert(g, s):
        src = mine if g == 0 else other
        size = (fs if g == 0 else fs_other)[0:1, :]
        block = lax.broadcasted_iota(jnp.int32, (1, KH), 1) // TR + xh * (KH // TR)
        keep = block < size

        def step(i, _):
            at = pl.multiple_of(i * 16, 16)
            v = jnp.where(keep, src[s, pl.ds(at, 16), :], 0.0)
            hi = v.astype(BF16)
            split[g, s, pl.ds(at, 16), :] = hi
            split[g, s, pl.ds(TR + at, 16), :] = (v - hi.astype(F32)).astype(BF16)
            return 0

        lax.fori_loop(0, TR // 16, step, 0)

    twin_queue = []

    def take(s):
        to_twin(s)
        convert(0, s)
        twin_queue.append(s)
        if len(twin_queue) > 4:
            drain()

    def drain():
        t = twin_queue.pop(0)
        from_twin(t)
        convert(1, t)

    plan(0)
    def drain_all():
        while twin_queue:
            drain()

    fs_copy.wait_recv()
    for c, load in zip((0, 1, 2, 3), loads):
        load.wait()
        take(slot(0, 0, c))
    for i in range(4):
        c, d = (0, 1, 2, 3)[i], (2, 3, 0, 1)[i]
        arrived(slot(0, 3, c))
        if c < 2:
            send_z(mine.at[slot(0, 3, c)], 0, 2, c, up)
        take(slot(0, 3, c))
        arrived(slot(0, 1, d))
        if d >= 2:
            send_z(mine.at[slot(0, 1, d)], 0, 2, d, down)
        take(slot(0, 1, d))
        if i == 3:
            code_copy.wait()
            drain_all()
            products(0, 0)
            products(1, 0)
        e = (0, 2, 1, 3)[i]
        s = slot(1, 0, e)
        arrived(s)
        send_z(mine.at[s], 1, 3, e, up)
        send_z(mine.at[s], 1, 1, e, down)
        take(s)
        if i == 0:
            plan(1)
        if i == 1:
            code_copy = pltpu.make_async_copy(codes, code_s, local.at[8])
            code_copy.start()
    for e in (0, 2, 1, 3):
        arrived(slot(0, 2, e))
        take(slot(0, 2, e))
    drain_all()
    for e in (0, 2, 1, 3):
        s = slot(1, 3, e)
        arrived(s)
        if e < 2:
            send_z(mine.at[s], 1, 2, e, up)
        take(s)
        s = slot(1, 1, e)
        arrived(s)
        if e >= 2:
            send_z(mine.at[s], 1, 2, e, down)
        take(s)
        if e == 0:
            products(0, 1)
        if e == 2:
            products(1, 1)
            drain_all()
        if e == 1:
            products(0, 2)
        if e == 3:
            products(1, 2)
    drain_all()
    products(0, 3)
    for e in (0, 2):
        arrived(slot(1, 2, e))
        take(slot(1, 2, e))
    products(1, 3)
    drain_all()
    products(0, 4)
    for e in (1, 3):
        arrived(slot(1, 2, e))
        take(slot(1, 2, e))
    products(1, 4)
    drain_all()
    for copy in sent:
        copy.wait_send()


def tiles_kernel(codes, rest, totals, held, reused, staged, acc, flat):
    def clear(i, _):
        acc[i] = jnp.zeros((TR, TR), F32)
        return 0

    lax.fori_loop(0, TRASH + 1, clear, 0)
    count = 0
    for g in range(2):
        def entry(k, _):
            flat[count + k] = rest[g, k] + (g << 18)
            return 0

        lax.fori_loop(0, totals[g * 8 + LEVELS, 0], entry, 0)
        count = count + totals[g * 8 + LEVELS, 0]

    def blank(k, _):
        flat[k] = TRASH
        return 0

    lax.fori_loop(count, jnp.maximum(count + UNROLL, MERGED * UNROLL), blank, 0)

    def add(g, n, t, value):
        at = jnp.where(t < totals[g * 8 + n, 0], codes[g * 8 + n, t] & 255, TRASH)
        acc[at] += value

    def fixed(g, n, first, again, base, per, i, u):
        t = first + i * per + u
        if again:
            add(g, n, t, reused[base + i * (per // 4) + u // 4, :, pl.ds((u % 4) * TR, TR)])
        else:
            add(g, n, t, staged[g, base + i * per + u])

    def rest_tile(t):
        c = flat[t]
        g, b, a, at = c >> 18, (c >> 13) & 31, (c >> 8) & 31, c & 255
        d = lax.dot_general(
            held[g, a], held[g, b], (((1,), (1,)), ((), ())), preferred_element_type=F32
        )
        return at, d

    def put(at, d):
        acc[at] += d[:TR, :TR] + (d[:TR, TR:] + d[TR:, :TR])

    runs, odd = [], []
    for g in range(2):
        for n, first, many, again, base in homes(g):
            grain = 4 * MERGED if again else MERGED
            even = many // grain * grain
            runs += [(g, n, first, again, base, even // MERGED, u) for u in range(even // MERGED)]
            odd += [(g, n, first + t, again, base + (t // 4 if again else t), t % 4 if again else 0) for t in range(even, many)]

    def merged(i, _):
        share = -(-len(runs) // UNROLL)
        for k in range(UNROLL):
            at, d = rest_tile(i * UNROLL + k)
            for g, n, first, again, base, per, u in runs[k * share : (k + 1) * share]:
                fixed(g, n, first, again, base, per, i, u)
            put(at, d)
        return 0

    lax.fori_loop(0, MERGED, merged, 0)
    for g, n, t, again, place, lane in odd:
        add(g, n, t, reused[place, :, pl.ds(lane * TR, TR)] if again else staged[g, place])

    def several(i, _):
        for k in range(UNROLL):
            put(*rest_tile(i * UNROLL + k))
        return 0

    lax.fori_loop(MERGED, (count + UNROLL - 1) // UNROLL, several, 0)


def scatter_kernel(
    part, out, opp, near, fwd, mid, mid_opp, mid_near, mid_fwd,
    send_sem, recv_sem,
):
    p = position()
    x = p["xh"] * 2 + p["xl"]

    def along_x(d):
        n = (x + d) % 4
        return device(p, xh=n // 2, xl=n % 2)

    def along_y(d):
        return device(p, y=(p["y"] + d) % 4)

    barrier = pltpu.get_barrier_semaphore()
    for to in (along_x(1), along_x(3), along_y(1), along_y(3)):
        pl.semaphore_signal(barrier, inc=1, device_id=to, device_id_type=MESH)
    pl.semaphore_wait(barrier, 4)

    sent = []
    count = [0]

    def send(src, dst, to):
        k = count[0]
        count[0] += 1
        copy = pltpu.make_async_remote_copy(
            src_ref=src, dst_ref=dst, send_sem=send_sem.at[k], recv_sem=recv_sem.at[k],
            device_id=to, device_id_type=MESH,
        )
        copy.start()
        sent.append(copy)
        return copy

    def begin(src, n, h, to, opp, near):
        half = n // 2
        o_up = send(src(2, 0, half), opp.at[h, 0], to(1))
        o_down = send(src(2, half, half), opp.at[h, 1], to(3))
        n_up = send(src(1, half, half), near.at[h, 0, pl.ds(half, half)], to(1))
        n_down = send(src(3, 0, half), near.at[h, 1, pl.ds(0, half)], to(3))
        return o_up, o_down, n_up, n_down

    def relay(copies, val, h, to):
        late = []
        copies[0].wait_recv()
        for lo in (4, 0):
            fwd[h, 0, pl.ds(lo, 4)] = val(1, lo, 4) + opp[h, 0, pl.ds(lo, 4)]
            late.append(send(fwd.at[h, 0, pl.ds(lo, 4)], near.at[h, 0, pl.ds(lo, 4)], to(1)))
        copies[1].wait_recv()
        for lo in (0, 4):
            fwd[h, 1, pl.ds(lo, 4)] = val(3, 8 + lo, 4) + opp[h, 1, pl.ds(lo, 4)]
            late.append(send(fwd.at[h, 1, pl.ds(lo, 4)], near.at[h, 1, pl.ds(8 + lo, 4)], to(3)))
        return [copies[2], copies[3]] + late

    ways = ((along_y, along_x), (along_x, along_y))

    def value(h):
        return lambda r, lo, size: part[pl.ds(h * 64 + r * 16 + lo, size)]

    firsts = []
    for h in range(2):
        firsts.append(
            begin(lambda r, lo, size: part.at[pl.ds(h * 64 + r * 16 + lo, size)], 16, h, ways[h][0], opp, near)
        )
    for h in range(2):
        firsts[h] = relay(firsts[h], value(h), h, ways[h][0])

    def settle(h, r):
        at = pl.ds(r * 4, 4)
        mid[h, at] = part[pl.ds(h * 64 + r * 4, 4)] + (near[h, 0, at] + near[h, 1, at])

    seconds = []
    for h in range(2):
        to = ways[h][1]
        n_up, n_down, up_1, up_0, down_2, down_3 = firsts[h]
        n_up.wait_recv()
        n_down.wait_recv()
        down_2.wait_recv()
        settle(h, 2)
        two = [
            send(mid.at[h, pl.ds(8, 2)], mid_opp.at[h, 0], to(1)),
            send(mid.at[h, pl.ds(10, 2)], mid_opp.at[h, 1], to(3)),
        ]
        up_1.wait_recv()
        settle(h, 1)
        two.append(send(mid.at[h, pl.ds(6, 2)], mid_near.at[h, 0, pl.ds(2, 2)], to(1)))
        seconds.append(two)
    for h in range(2):
        to = ways[h][1]
        n_up, n_down, up_1, up_0, down_2, down_3 = firsts[h]
        down_3.wait_recv()
        settle(h, 3)
        seconds[h].append(send(mid.at[h, pl.ds(12, 2)], mid_near.at[h, 1, pl.ds(0, 2)], to(3)))
    ends = []
    for h in range(2):
        to = ways[h][1]
        o_up, o_down, n_up, n_down = seconds[h]
        o_up.wait_recv()
        mid_fwd[h, 0] = mid[h, pl.ds(4, 2)] + mid_opp[h, 0]
        f_up = send(mid_fwd.at[h, 0], mid_near.at[h, 0, pl.ds(0, 2)], to(1))
        o_down.wait_recv()
        mid_fwd[h, 1] = mid[h, pl.ds(14, 2)] + mid_opp[h, 1]
        f_down = send(mid_fwd.at[h, 1], mid_near.at[h, 1, pl.ds(2, 2)], to(3))
        ends.append((n_up, n_down, f_up, f_down))
    for h in range(2):
        firsts[h][3].wait_recv()
        settle(h, 0)
    for h in range(2):
        for copy in ends[h]:
            copy.wait_recv()
        out[pl.ds(h * 4, 4)] = mid[h, pl.ds(0, 4)] + (mid_near[h, 0] + mid_near[h, 1])
    for copy in sent:
        copy.wait_send()


def per_device(factor_rows, front_sizes, tile_counts, parent_tiles, parent_entries):
    vmem = pl.BlockSpec(memory_space=pltpu.VMEM)
    smem = pl.BlockSpec(memory_space=pltpu.SMEM)
    dma = pltpu.SemaphoreType.DMA
    hbm = pl.BlockSpec(memory_space=pltpu.HBM)

    def in_hbm(a):
        return pltpu.with_memory_space_constraint(a, pltpu.HBM)

    split, reused, staged, codes, rest, totals = pl.pallas_call(
        gather_kernel,
        out_shape=(
            jax.ShapeDtypeStruct((2, EB, 2 * TR, KH), BF16),
            jax.ShapeDtypeStruct((EB, TR, KH), F32),
            jax.ShapeDtypeStruct((2, STAGED, TR, TR), F32),
            jax.ShapeDtypeStruct((16, 128), jnp.int32),
            jax.ShapeDtypeStruct((8, REST), jnp.int32),
            jax.ShapeDtypeStruct((16, 128), jnp.int32),
        ),
        in_specs=[hbm, hbm, smem, hbm],
        out_specs=(vmem,) * 6,
        scratch_shapes=[
            pltpu.VMEM((EB, TR, KH), F32),
            pltpu.VMEM((8, KH), jnp.int32),
            pltpu.VMEM((8, KH), jnp.int32),
            pltpu.VMEM((2, EB, EB), jnp.int32),
            pltpu.SMEM((16,), jnp.int32),
            pltpu.SMEM((16, 128), jnp.int32),
            pltpu.VMEM((REST, 128), F32),
            dma((4,)),
            dma((24,)),
            dma((32,)),
            dma((32,)),
            dma((32,)),
            dma((9,)),
            dma((2,)),
        ],
        compiler_params=pltpu.CompilerParams(collective_id=0, has_side_effects=True, vmem_limit_bytes=10 * 2**20),
        name="gather",
    )(in_hbm(factor_rows[0]), in_hbm(parent_tiles), front_sizes, in_hbm(tile_counts))
    part = pl.pallas_call(
        tiles_kernel,
        out_shape=jax.ShapeDtypeStruct((TRASH + 1, TR, TR), F32),
        in_specs=[smem, smem, smem, vmem, vmem, vmem],
        out_specs=vmem,
        scratch_shapes=[pltpu.SMEM((2 * REST + MERGED * UNROLL,), jnp.int32)],
        compiler_params=pltpu.CompilerParams(vmem_limit_bytes=4 * 2**20),
        name="tiles",
    )(codes, rest, totals, split, reused, staged)
    summed = pl.pallas_call(
        scatter_kernel,
        out_shape=jax.ShapeDtypeStruct((8, TR, TR), F32),
        in_specs=[vmem],
        out_specs=vmem,
        scratch_shapes=[
            pltpu.VMEM((2, 2, 8, TR, TR), F32),
            pltpu.VMEM((2, 2, 16, TR, TR), F32),
            pltpu.VMEM((2, 2, 8, TR, TR), F32),
            pltpu.VMEM((2, 16, TR, TR), F32),
            pltpu.VMEM((2, 2, 2, TR, TR), F32),
            pltpu.VMEM((2, 2, 4, TR, TR), F32),
            pltpu.VMEM((2, 2, 2, TR, TR), F32),
            dma((28,)),
            dma((28,)),
        ],
        compiler_params=pltpu.CompilerParams(collective_id=1, has_side_effects=True, vmem_limit_bytes=14 * 2**20),
        name="scatter",
    )(part)
    return parent_entries - summed


def solution(mesh):
    in_specs = (P("front", "blk", None), P("front"), P(), P(), P(("front", "blk"), None, None))
    out_specs = P(("front", "blk"), None, None)
    return jax.shard_map(
        per_device, mesh=mesh, in_specs=in_specs, out_specs=out_specs, check_vma=False
    )
```

```python
import functools

import jax
import jax.numpy as jnp
from jax import lax
from jax.experimental import pallas as pl
from jax.experimental.pallas import tpu as pltpu
from jax.sharding import PartitionSpec as P

TR = 128
KH = 512
CB = 4
EB = 32
UNROLL = 8
MERGED = 4
FIXED = (16, 32, 24, 28, 20)
LEVELS = len(FIXED)
STAGED = 64
REST = 256
TRASH = 128

MESH = pl.DeviceIdType.MESH
F32 = jnp.float32
BF16 = jnp.bfloat16


def homes(g):
    return (
        (0, 0, 16, True, g * 4),
        (1, 0, 24, True, 8 + g * 6),
        (1, 24, 8, False, 0),
        (2, 0, 24, False, 8),
        (3, 0, 28, False, 32),
        (4, 0, 16, True, 20 + g * 8),
        (4, 16, 4, False, 60),
    )


def position():
    front, blk = lax.axis_index("front"), lax.axis_index("blk")
    return dict(
        front=front,
        blk=blk,
        y=front // 4,
        xl=(front // 2) % 2,
        core=front % 2,
        xh=blk // 4,
        z=blk % 4,
    )


def device(p, **moves):
    q = {**p, **moves}
    return {"front": q["y"] * 4 + q["xl"] * 2 + q["core"], "blk": q["xh"] * 4 + q["z"]}


def slot(xs, dz, c):
    return (xs * 4 + dz) * CB + c


def gather_kernel(
    x, parents, sizes, counts, split, other, staged, codes, rest, totals,
    mine, fs, fs_other, targets, count_s, code_s, rows_by_place,
    x_send, z_send, recv, core_send, core_recv, local, fs_sem,
):
    p = position()
    z, xh = p["z"], p["xh"]
    up, down = device(p, z=(z + 1) % 4), device(p, z=(z + 3) % 4)
    across = device(p, xh=1 - xh)
    twin = device(p, core=1 - p["core"])

    fronts = [(p["front"] // 2) * 2 + (p["core"] if g == 0 else 1 - p["core"]) for g in range(2)]
    small = [
        pltpu.make_async_copy(counts, count_s, local.at[5]),
        pltpu.make_async_copy(parents.at[fronts[0]], targets.at[0], local.at[6]),
        pltpu.make_async_copy(parents.at[fronts[1]], targets.at[1], local.at[7]),
    ]
    for copy in small:
        copy.start()
    barrier = pltpu.get_barrier_semaphore()
    for other_dev in (up, down, across, twin):
        pl.semaphore_signal(barrier, inc=1, device_id=other_dev, device_id_type=MESH)
    pl.semaphore_wait(barrier, 4)

    sent = []

    def send(src, dst, ssem, rsem, to):
        copy = pltpu.make_async_remote_copy(
            src_ref=src, dst_ref=dst, send_sem=ssem, recv_sem=rsem, device_id=to, device_id_type=MESH
        )
        copy.start()
        sent.append(copy)

    n_z = [0]

    def send_z(src, xs, dz, c, to):
        s = slot(xs, dz, c)
        send(src, mine.at[s], z_send.at[n_z[0]], recv.at[s], to)
        n_z[0] += 1

    def arrived(s):
        pltpu.make_async_remote_copy(
            src_ref=mine.at[s], dst_ref=mine.at[s], send_sem=z_send.at[0], recv_sem=recv.at[s],
            device_id=up, device_id_type=MESH,
        ).wait_recv()

    def to_twin(s):
        send(mine.at[s], other.at[s], core_send.at[s], core_recv.at[s], twin)

    def from_twin(s):
        pltpu.make_async_remote_copy(
            src_ref=mine.at[s], dst_ref=other.at[s], send_sem=core_send.at[s], recv_sem=core_recv.at[s],
            device_id=twin, device_id_type=MESH,
        ).wait_recv()

    own_cols = pl.ds(pl.multiple_of(xh * KH, KH), KH)
    across_cols = pl.ds(pl.multiple_of((1 - xh) * KH, KH), KH)

    def rows(c):
        return pl.ds(c * TR, TR)

    fs[...] = jnp.full((8, KH), sizes[0], jnp.int32)
    loads = []
    for c, d in ((0, 2), (1, 3), (2, 0), (3, 1)):
        send_z(x.at[rows(c), own_cols], 0, 3, c, up)
        send_z(x.at[rows(d), own_cols], 0, 1, d, down)
        load = pltpu.make_async_copy(x.at[rows(c), own_cols], mine.at[slot(0, 0, c)], local.at[c])
        load.start()
        loads.append(load)

    for c in (0, 2, 1, 3):
        s = slot(1, 0, c)
        send(x.at[rows(c), across_cols], mine.at[s], x_send.at[c], recv.at[s], across)
    for copy in small:
        copy.wait()
    send(fs, fs_other, fs_sem.at[0], fs_sem.at[1], twin)
    fs_copy = sent[-1]

    col = lax.broadcasted_iota(jnp.int32, (EB, EB), 1)
    row = lax.broadcasted_iota(jnp.int32, (EB, EB), 0)
    lower = (row >= col).astype(F32)
    before = (row < col).astype(F32)

    def place_of(block):
        return ((((block >> 4) ^ xh) << 4) + ((((block >> 2) - z) & 3) << 2)) + (block & 3)

    def level_of(s):
        early = jnp.where((s < 8) | ((s >= 12) & (s < 16)), 0, 1)
        return jnp.where(s < 20, early, jnp.where((s >= 24) & (s < 28), 4, 2) + (s & 1))

    a_slot, b_slot = place_of(row), place_of(col)
    level = jnp.maximum(level_of(a_slot), level_of(b_slot))

    def places(hit):
        rank = jnp.dot(lower, hit.astype(F32), preferred_element_type=F32)
        many = jnp.broadcast_to(rank[EB - 1 : EB, :], (8, EB))
        start = jnp.dot(many, before, preferred_element_type=F32)
        at = (rank + start[0:1, :]).astype(jnp.int32) - 1
        return jnp.where(hit, at, -1), jnp.sum(many[0:1, :], axis=1, keepdims=True).astype(jnp.int32)

    ones = jnp.full((8, EB), 1.0, F32)

    def listed(at, code, size):
        def eight(i, _):
            first = pl.multiple_of(i * 8, 8)
            for k in range(8):
                rows_by_place[pl.ds(first + k, 1), 0:EB] = jnp.sum(
                    jnp.where(at == first + k, code, 0.0), axis=0, keepdims=True
                )
            return 0

        whole = (size + 7) // 8 * 8
        lax.fori_loop(0, whole // 8, eight, 0)
        found = lax.dot_general(
            ones, rows_by_place[0:whole, 0:EB], (((1,), (1,)), ((), ())),
            precision=lax.Precision.HIGHEST, preferred_element_type=F32,
        )
        return found[0:1, 0:size].astype(jnp.int32)

    def plan(g):
        target = targets[g]
        live = count_s[fronts[g]]
        dest = target >> 3
        dest_front, dest_blk = dest >> 3, dest & 7
        hit = ((dest_blk & 3) == z) & ((dest_front & 1) == p["core"])
        hit = hit & (row < live) & (col < live)
        rx = ((dest_blk >> 2) * 2 + ((dest_front >> 1) & 1) - (p["xh"] * 2 + p["xl"])) & 3
        ry = ((dest_front >> 2) - p["y"]) & 3
        place = target & 7
        first = place < 4
        at = jnp.where(first, ry * 4 + rx, 16 + rx * 4 + ry) * 4 + (place & 3)
        code = ((b_slot << 13) + (a_slot << 8) + at).astype(F32)
        late = hit & (level == LEVELS)
        over = hit & (level < 0)
        for n in range(LEVELS):
            where, many = places((hit & (level == n)) | over)
            codes[g * 8 + n : g * 8 + n + 1, 0 : FIXED[n]] = listed(where, code, FIXED[n])
            totals[g * 8 + n : g * 8 + n + 1, :] = jnp.broadcast_to(many, (1, 128))
            over = where >= FIXED[n]
        where, many = places(late | over)
        rest[g : g + 1, :] = listed(where, code, REST)
        totals[g * 8 + LEVELS : g * 8 + LEVELS + 1, :] = jnp.broadcast_to(many, (1, 128))

    def product(g, n, t):
        c = code_s[g * 8 + n, t]
        d = lax.dot_general(
            split[g, (c >> 8) & 31], split[g, (c >> 13) & 31], (((1,), (1,)), ((), ())),
            preferred_element_type=F32,
        )
        return d[:TR, :TR] + (d[:TR, TR:] + d[TR:, :TR])

    def products(g, n):
        for level_, first, many, again, base in homes(g):
            if level_ == n:
                for t in range(many):
                    d = product(g, n, first + t)
                    if again:
                        other[base + t // 4, :, pl.ds((t % 4) * TR, TR)] = d
                    else:
                        staged[g, base + t] = d

    def convert(g, s):
        src = mine if g == 0 else other
        size = (fs if g == 0 else fs_other)[0:1, :]
        block = lax.broadcasted_iota(jnp.int32, (1, KH), 1) // TR + xh * (KH // TR)
        keep = block < size

        def step(i, _):
            at = pl.multiple_of(i * 16, 16)
            v = jnp.where(keep, src[s, pl.ds(at, 16), :], 0.0)
            hi = v.astype(BF16)
            split[g, s, pl.ds(at, 16), :] = hi
            split[g, s, pl.ds(TR + at, 16), :] = (v - hi.astype(F32)).astype(BF16)
            return 0

        lax.fori_loop(0, TR // 16, step, 0)

    twin_queue = []

    def take(s):
        to_twin(s)
        convert(0, s)
        twin_queue.append(s)
        if len(twin_queue) > 4:
            drain()

    def drain():
        t = twin_queue.pop(0)
        from_twin(t)
        convert(1, t)

    plan(0)
    def drain_all():
        while twin_queue:
            drain()

    fs_copy.wait_recv()
    for c, load in zip((0, 1, 2, 3), loads):
        load.wait()
        take(slot(0, 0, c))
    for i in range(4):
        c, d = (0, 1, 2, 3)[i], (2, 3, 0, 1)[i]
        arrived(slot(0, 3, c))
        if c < 2:
            send_z(mine.at[slot(0, 3, c)], 0, 2, c, up)
        take(slot(0, 3, c))
        arrived(slot(0, 1, d))
        if d >= 2:
            send_z(mine.at[slot(0, 1, d)], 0, 2, d, down)
        take(slot(0, 1, d))
        if i == 3:
            code_copy.wait()
            drain_all()
            products(0, 0)
            products(1, 0)
        e = (0, 2, 1, 3)[i]
        s = slot(1, 0, e)
        arrived(s)
        send_z(mine.at[s], 1, 3, e, up)
        send_z(mine.at[s], 1, 1, e, down)
        take(s)
        if i == 0:
            plan(1)
        if i == 1:
            code_copy = pltpu.make_async_copy(codes, code_s, local.at[8])
            code_copy.start()
    for e in (0, 2, 1, 3):
        arrived(slot(0, 2, e))
        take(slot(0, 2, e))
    drain_all()
    for e in (0, 2, 1, 3):
        s = slot(1, 3, e)
        arrived(s)
        if e < 2:
            send_z(mine.at[s], 1, 2, e, up)
        take(s)
        s = slot(1, 1, e)
        arrived(s)
        if e >= 2:
            send_z(mine.at[s], 1, 2, e, down)
        take(s)
        if e == 0:
            products(0, 1)
        if e == 2:
            products(1, 1)
            drain_all()
        if e == 1:
            products(0, 2)
        if e == 3:
            products(1, 2)
    drain_all()
    products(0, 3)
    for e in (0, 2):
        arrived(slot(1, 2, e))
        take(slot(1, 2, e))
    products(1, 3)
    drain_all()
    products(0, 4)
    for e in (1, 3):
        arrived(slot(1, 2, e))
        take(slot(1, 2, e))
    products(1, 4)
    drain_all()
    for copy in sent:
        copy.wait_send()


def tiles_kernel(codes, rest, totals, held, reused, staged, acc, flat):
    def clear(i, _):
        acc[i] = jnp.zeros((TR, TR), F32)
        return 0

    lax.fori_loop(0, TRASH + 1, clear, 0)
    count = 0
    for g in range(2):
        def entry(k, _):
            flat[count + k] = rest[g, k] + (g << 18)
            return 0

        lax.fori_loop(0, totals[g * 8 + LEVELS, 0], entry, 0)
        count = count + totals[g * 8 + LEVELS, 0]

    def blank(k, _):
        flat[k] = TRASH
        return 0

    lax.fori_loop(count, jnp.maximum(count + UNROLL, MERGED * UNROLL), blank, 0)

    def add(g, n, t, value):
        at = jnp.where(t < totals[g * 8 + n, 0], codes[g * 8 + n, t] & 255, TRASH)
        acc[at] += value

    def fixed(g, n, first, again, base, per, i, u):
        t = first + i * per + u
        if again:
            add(g, n, t, reused[base + i * (per // 4) + u // 4, :, pl.ds((u % 4) * TR, TR)])
        else:
            add(g, n, t, staged[g, base + i * per + u])

    def rest_tile(t):
        c = flat[t]
        g, b, a, at = c >> 18, (c >> 13) & 31, (c >> 8) & 31, c & 255
        d = lax.dot_general(
            held[g, a], held[g, b], (((1,), (1,)), ((), ())), preferred_element_type=F32
        )
        return at, d

    def put(at, d):
        acc[at] += d[:TR, :TR] + (d[:TR, TR:] + d[TR:, :TR])

    runs, odd = [], []
    for g in range(2):
        for n, first, many, again, base in homes(g):
            grain = 4 * MERGED if again else MERGED
            even = many // grain * grain
            runs += [(g, n, first, again, base, even // MERGED, u) for u in range(even // MERGED)]
            odd += [(g, n, first + t, again, base + (t // 4 if again else t), t % 4 if again else 0) for t in range(even, many)]

    def merged(i, _):
        share = -(-len(runs) // UNROLL)
        for k in range(UNROLL):
            at, d = rest_tile(i * UNROLL + k)
            for g, n, first, again, base, per, u in runs[k * share : (k + 1) * share]:
                fixed(g, n, first, again, base, per, i, u)
            put(at, d)
        return 0

    lax.fori_loop(0, MERGED, merged, 0)
    for g, n, t, again, place, lane in odd:
        add(g, n, t, reused[place, :, pl.ds(lane * TR, TR)] if again else staged[g, place])

    def several(i, _):
        for k in range(UNROLL):
            put(*rest_tile(i * UNROLL + k))
        return 0

    lax.fori_loop(MERGED, (count + UNROLL - 1) // UNROLL, several, 0)


def scatter_kernel(
    part, entries, out, opp, near, fwd, mid, mid_opp, mid_near, mid_fwd,
    send_sem, recv_sem,
):
    p = position()
    x = p["xh"] * 2 + p["xl"]

    def along_x(d):
        n = (x + d) % 4
        return device(p, xh=n // 2, xl=n % 2)

    def along_y(d):
        return device(p, y=(p["y"] + d) % 4)

    barrier = pltpu.get_barrier_semaphore()
    for to in (along_x(1), along_x(3), along_y(1), along_y(3)):
        pl.semaphore_signal(barrier, inc=1, device_id=to, device_id_type=MESH)
    pl.semaphore_wait(barrier, 4)

    sent = []
    count = [0]

    def send(src, dst, to):
        k = count[0]
        count[0] += 1
        copy = pltpu.make_async_remote_copy(
            src_ref=src, dst_ref=dst, send_sem=send_sem.at[k], recv_sem=recv_sem.at[k],
            device_id=to, device_id_type=MESH,
        )
        copy.start()
        sent.append(copy)
        return copy

    def begin(src, n, h, to, opp, near):
        half = n // 2
        o_up = send(src(2, 0, half), opp.at[h, 0], to(1))
        o_down = send(src(2, half, half), opp.at[h, 1], to(3))
        n_up = send(src(1, half, half), near.at[h, 0, pl.ds(half, half)], to(1))
        n_down = send(src(3, 0, half), near.at[h, 1, pl.ds(0, half)], to(3))
        return o_up, o_down, n_up, n_down

    def relay(copies, val, h, to):
        late = []
        copies[0].wait_recv()
        for lo in (4, 0):
            fwd[h, 0, pl.ds(lo, 4)] = val(1, lo, 4) + opp[h, 0, pl.ds(lo, 4)]
            late.append(send(fwd.at[h, 0, pl.ds(lo, 4)], near.at[h, 0, pl.ds(lo, 4)], to(1)))
        copies[1].wait_recv()
        for lo in (0, 4):
            fwd[h, 1, pl.ds(lo, 4)] = val(3, 8 + lo, 4) + opp[h, 1, pl.ds(lo, 4)]
            late.append(send(fwd.at[h, 1, pl.ds(lo, 4)], near.at[h, 1, pl.ds(8 + lo, 4)], to(3)))
        return [copies[2], copies[3]] + late

    ways = ((along_y, along_x), (along_x, along_y))

    def value(h):
        return lambda r, lo, size: part[pl.ds(h * 64 + r * 16 + lo, size)]

    firsts = []
    for h in range(2):
        firsts.append(
            begin(lambda r, lo, size: part.at[pl.ds(h * 64 + r * 16 + lo, size)], 16, h, ways[h][0], opp, near)
        )
    for h in range(2):
        firsts[h] = relay(firsts[h], value(h), h, ways[h][0])

    def settle(h, r):
        at = pl.ds(r * 4, 4)
        mid[h, at] = part[pl.ds(h * 64 + r * 4, 4)] + (near[h, 0, at] + near[h, 1, at])

    seconds = []
    for h in range(2):
        to = ways[h][1]
        n_up, n_down, up_1, up_0, down_2, down_3 = firsts[h]
        n_up.wait_recv()
        n_down.wait_recv()
        down_2.wait_recv()
        settle(h, 2)
        two = [
            send(mid.at[h, pl.ds(8, 2)], mid_opp.at[h, 0], to(1)),
            send(mid.at[h, pl.ds(10, 2)], mid_opp.at[h, 1], to(3)),
        ]
        up_1.wait_recv()
        settle(h, 1)
        two.append(send(mid.at[h, pl.ds(6, 2)], mid_near.at[h, 0, pl.ds(2, 2)], to(1)))
        seconds.append(two)
    for h in range(2):
        to = ways[h][1]
        n_up, n_down, up_1, up_0, down_2, down_3 = firsts[h]
        down_3.wait_recv()
        settle(h, 3)
        seconds[h].append(send(mid.at[h, pl.ds(12, 2)], mid_near.at[h, 1, pl.ds(0, 2)], to(3)))
    ends = []
    for h in range(2):
        to = ways[h][1]
        o_up, o_down, n_up, n_down = seconds[h]
        o_up.wait_recv()
        mid_fwd[h, 0] = mid[h, pl.ds(4, 2)] + mid_opp[h, 0]
        f_up = send(mid_fwd.at[h, 0], mid_near.at[h, 0, pl.ds(0, 2)], to(1))
        o_down.wait_recv()
        mid_fwd[h, 1] = mid[h, pl.ds(14, 2)] + mid_opp[h, 1]
        f_down = send(mid_fwd.at[h, 1], mid_near.at[h, 1, pl.ds(2, 2)], to(3))
        ends.append((n_up, n_down, f_up, f_down))
    for h in range(2):
        firsts[h][3].wait_recv()
        settle(h, 0)
    for h in range(2):
        for copy in ends[h]:
            copy.wait_recv()
        out[pl.ds(h * 4, 4)] = entries[pl.ds(h * 4, 4)] - (mid[h, pl.ds(0, 4)] + (mid_near[h, 0] + mid_near[h, 1]))
    for copy in sent:
        copy.wait_send()


def per_device(factor_rows, front_sizes, tile_counts, parent_tiles, parent_entries):
    vmem = pl.BlockSpec(memory_space=pltpu.VMEM)
    smem = pl.BlockSpec(memory_space=pltpu.SMEM)
    dma = pltpu.SemaphoreType.DMA
    hbm = pl.BlockSpec(memory_space=pltpu.HBM)

    def in_hbm(a):
        return pltpu.with_memory_space_constraint(a, pltpu.HBM)

    split, reused, staged, codes, rest, totals = pl.pallas_call(
        gather_kernel,
        out_shape=(
            jax.ShapeDtypeStruct((2, EB, 2 * TR, KH), BF16),
            jax.ShapeDtypeStruct((EB, TR, KH), F32),
            jax.ShapeDtypeStruct((2, STAGED, TR, TR), F32),
            jax.ShapeDtypeStruct((16, 128), jnp.int32),
            jax.ShapeDtypeStruct((8, REST), jnp.int32),
            jax.ShapeDtypeStruct((16, 128), jnp.int32),
        ),
        in_specs=[hbm, hbm, smem, hbm],
        out_specs=(vmem,) * 6,
        scratch_shapes=[
            pltpu.VMEM((EB, TR, KH), F32),
            pltpu.VMEM((8, KH), jnp.int32),
            pltpu.VMEM((8, KH), jnp.int32),
            pltpu.VMEM((2, EB, EB), jnp.int32),
            pltpu.SMEM((16,), jnp.int32),
            pltpu.SMEM((16, 128), jnp.int32),
            pltpu.VMEM((REST, 128), F32),
            dma((4,)),
            dma((24,)),
            dma((32,)),
            dma((32,)),
            dma((32,)),
            dma((9,)),
            dma((2,)),
        ],
        compiler_params=pltpu.CompilerParams(collective_id=0, has_side_effects=True, vmem_limit_bytes=10 * 2**20),
        name="gather",
    )(in_hbm(factor_rows[0]), in_hbm(parent_tiles), front_sizes, in_hbm(tile_counts))
    part = pl.pallas_call(
        tiles_kernel,
        out_shape=jax.ShapeDtypeStruct((TRASH + 1, TR, TR), F32),
        in_specs=[smem, smem, smem, vmem, vmem, vmem],
        out_specs=vmem,
        scratch_shapes=[pltpu.SMEM((2 * REST + MERGED * UNROLL,), jnp.int32)],
        compiler_params=pltpu.CompilerParams(vmem_limit_bytes=4 * 2**20),
        name="tiles",
    )(codes, rest, totals, split, reused, staged)
    return pl.pallas_call(
        scatter_kernel,
        out_shape=jax.ShapeDtypeStruct((8, TR, TR), F32),
        in_specs=[vmem, vmem],
        out_specs=vmem,
        scratch_shapes=[
            pltpu.VMEM((2, 2, 8, TR, TR), F32),
            pltpu.VMEM((2, 2, 16, TR, TR), F32),
            pltpu.VMEM((2, 2, 8, TR, TR), F32),
            pltpu.VMEM((2, 16, TR, TR), F32),
            pltpu.VMEM((2, 2, 2, TR, TR), F32),
            pltpu.VMEM((2, 2, 4, TR, TR), F32),
            pltpu.VMEM((2, 2, 2, TR, TR), F32),
            dma((28,)),
            dma((28,)),
        ],
        compiler_params=pltpu.CompilerParams(collective_id=1, has_side_effects=True, vmem_limit_bytes=14 * 2**20),
        name="scatter",
    )(part, parent_entries)


def solution(mesh):
    in_specs = (P("front", "blk", None), P("front"), P(), P(), P(("front", "blk"), None, None))
    out_specs = P(("front", "blk"), None, None)
    return jax.shard_map(
        per_device, mesh=mesh, in_specs=in_specs, out_specs=out_specs, check_vma=False
    )
```
